256 devices in a mesh: layer: 32 (over y_lo, z, core), col: 4 (over x), row: 2 (over y_hi).
Axes of the slice: x: 4, y: 4 (y_hi: 2, y_lo: 2; y = y_hi * 2 + y_lo), z: 8, core: 2. Of those that a mesh axis runs over, the one named last changes fastest.
Arguments:
- front_copies: bfloat16 [32, 3072, 3072], P('layer', 'row', 'col'), may hold values from -6 to 6
- lower_panels: bfloat16 [32, 2, 3072, 512], P('layer', None, 'row', 'col'), may hold values from -0.25 to 0.25
- upper_panels: bfloat16 [32, 2, 512, 3072], P('layer', None, 'row', 'col'), may hold values from -6 to 6
- diag_blocks: float32 [32, 2, 512, 512], P('layer'), may hold values from -2 to 4, as said below
- block_fill: int32 [32, 2, 24], P('layer'), may hold values 0 or 1
- widths: int32 [32, 2], P('layer'), may hold values from 256 to 512, as said below
Outputs:
- summed_strips: float32 [32, 384, 3072], P('layer', 'row', 'col')
The draws below stay inside these ranges and needn't reach their ends.
Inputs may be any that keep to these rules, and one draw needn't show every extreme that they name: `widths`: each supernode uses between half and all of its 512 columns; some supernode uses all. `diag_blocks`: diagonal entries lie between 1 and 4.
All inputs are finite; a program needn't handle non-finite values. No bound on the sum of `block_fill` on one device may be relied on, other than what follows from the above.
Results may differ from the reference program's by a relative error of at most 0.0014.
Values may be sent and summed in bfloat16 or wider, within the bound.
No kernel may reach another device: no remote copies, remote signals or barrier semaphores. Data moves between devices by JAX's collectives and lax.ppermute only.
A program may use at most 320 MiB of HBM per device.

```python
import math
import jax
import jax.numpy as jnp
from jax import lax

F = 3072
W = 512
S = 2
BLOCK = 128
NS_ITERS = 3
NB = 24
LAYERS = 32
GROUP = 8
N_ROW = 2


def draw_diag_blocks(key, part):
    key_diag = jax.random.fold_in(key, 11)
    key_off = jax.random.fold_in(key, 12)
    diagonal = jax.random.uniform(key_diag, (LAYERS, S, W), jnp.float32, 0.0, 1.0)
    diagonal = jnp.exp(diagonal * math.log(4.0))
    coupling = jnp.clip(jax.random.normal(key_off, (LAYERS, S, W, W), jnp.float32), -4.0, 4.0)
    scaling = jnp.sqrt(diagonal[:, :, :, None] * diagonal[:, :, None, :]) * (0.6 / math.sqrt(W))
    indices = jnp.arange(W, dtype=jnp.int32)
    off_diag = indices[:, None] != indices[None, :]
    return jnp.where(off_diag, coupling * scaling, diagonal[:, :, :, None] * jnp.ones((1, 1, 1, W), jnp.float32))


def draw_widths(key, part):
    values = jax.random.randint(jax.random.fold_in(key, 21), (LAYERS, S), W // 2, W + 1, jnp.int32)
    values = values.at[0, 0].set(W)
    return values.at[0, 1].set(W // 2)


def plant(entries, rng, low, top_value):
    longest = entries.shape.index(max(entries.shape))
    spots = []
    for shift in (0, 1):
        where = [jax.random.randint(jax.random.fold_in(rng, axis), (), 0, length) for axis, length in enumerate(entries.shape)]
        where[longest] = (where[longest] + shift) % entries.shape[longest]
        spots.append(tuple(where))
    return entries.at[spots[0]].set(low).at[spots[1]].set(top_value)


def steps_of(key, extent, shards, least, largest):
    def one(axis_at, blocks):
        heights = jax.random.uniform(jax.random.fold_in(jax.random.fold_in(key, 6), axis_at), (blocks,), jnp.float32, least / len(shards), largest / len(shards))
        return jnp.repeat(jnp.exp(heights), extent[axis_at] // blocks).reshape((-1,) + (1,) * (len(extent) - axis_at - 1))

    loudness = one(*shards[0])
    for cut in shards[1:]:
        loudness = loudness * one(*cut)
    return loudness


def scatter_about(own_key, extent, deviation, bound, split=(), held_as=jnp.bfloat16):
    gain = steps_of(own_key, extent, split, -0.22, 0.18) if split else 1.0
    values = jax.random.normal(own_key, extent, jnp.float32) * deviation * gain
    return jnp.minimum(jnp.maximum(values, -bound), bound).astype(held_as)


def setup_inputs(seed: int = 0) -> dict:
    keys = jax.random.split(jax.random.key(seed), 7)
    front_copies = scatter_about(keys[0], (LAYERS, F, F), 1.0, 6.0, ((0, 32), (1, 2), (2, 4)))
    lower_panels = scatter_about(keys[1], (LAYERS, S, F, W), W ** -0.5, 0.25, ((0, 32), (2, 2), (3, 4)))
    upper_panels = scatter_about(keys[2], (LAYERS, S, W, F), 1.0, 6.0, ((0, 32), (2, 2), (3, 4)))
    diag_blocks = draw_diag_blocks(jax.random.fold_in(keys[6], 71), 0)
    block_fill = plant((jax.random.randint(keys[4], (LAYERS, S, NB), 0, 3) < 2).astype(jnp.int32), jax.random.fold_in(keys[4], 1), 0, 1)
    widths = draw_widths(jax.random.fold_in(keys[6], 71), 0)
    return dict(front_copies=front_copies, lower_panels=lower_panels, upper_panels=upper_panels, diag_blocks=diag_blocks, block_fill=block_fill, widths=widths)


def masked_system(system_in, width_vec):
    order = system_in.shape[-1]
    indices = jnp.arange(order, dtype=jnp.int32)
    inside = indices[None, :] < width_vec[:, None]
    square = inside[:, :, None] & inside[:, None, :]
    identity = jnp.eye(order, dtype=system_in.dtype)
    return jnp.where(square, system_in, identity[None]), square


def schulz_inverse(system):
    diagonal = jnp.diagonal(system, axis1=1, axis2=2)
    order = system.shape[-1]
    current = jnp.eye(order, dtype=system.dtype)[None] / diagonal[:, None, :]
    for sweep_no in range(NS_ITERS):
        product = jnp.einsum("sij,sjk->sik", system, current, precision=lax.Precision.HIGHEST)
        current = 2.0 * current - jnp.einsum("sij,sjk->sik", current, product, precision=lax.Precision.HIGHEST)
    return current


def layer_update(front, lower, upper, system_in, width_vec, fill):
    system, square = masked_system(system_in, width_vec)
    inverse = schulz_inverse(system)
    kept_inverse = jnp.where(square, inverse, 0.0)
    fill_mask = jnp.repeat(fill, BLOCK, axis=1).astype(jnp.float32)
    scaled = jnp.einsum("sij,sjk->sik", kept_inverse, upper.astype(jnp.float32), precision=lax.Precision.HIGHEST)
    scaled_upper = (scaled * fill_mask[:, None, :]).astype(jnp.bfloat16)
    masked_lower = lower * fill_mask[:, :, None].astype(jnp.bfloat16)
    update = jnp.zeros((F, F), jnp.float32)
    for member in range(S):
        update = update + jnp.dot(masked_lower[member], scaled_upper[member], preferred_element_type=jnp.float32)
    return front.astype(jnp.float32) - update


def reference(front_copies, lower_panels, upper_panels, diag_blocks, block_fill, widths):
    def group_strips(group_no):
        first = group_no * GROUP

        def accumulate(total, offset):
            layer_no = (first + offset).astype(jnp.int32)
            front = lax.dynamic_index_in_dim(front_copies, layer_no, 0, keepdims=False)
            lower = lax.dynamic_index_in_dim(lower_panels, layer_no, 0, keepdims=False)
            upper = lax.dynamic_index_in_dim(upper_panels, layer_no, 0, keepdims=False)
            system_in = lax.dynamic_index_in_dim(diag_blocks, layer_no, 0, keepdims=False)
            fill = lax.dynamic_index_in_dim(block_fill, layer_no, 0, keepdims=False)
            width_vec = lax.dynamic_index_in_dim(widths, layer_no, 0, keepdims=False)
            return total + layer_update(front, lower, upper, system_in, width_vec, fill), None

        total, unused = lax.scan(accumulate, jnp.zeros((F, F), jnp.float32), jnp.arange(GROUP, dtype=jnp.int32))
        strips = total.reshape(N_ROW, GROUP, F // (GROUP * N_ROW), F)
        return jnp.transpose(strips, (1, 0, 2, 3)).reshape(GROUP, F // GROUP, F)

    result = lax.map(group_strips, jnp.arange(LAYERS // GROUP, dtype=jnp.int32))
    return result.reshape(LAYERS, F // GROUP, F)
```

```python
import jax
import jax.numpy as jnp
from jax import lax
from jax.experimental import pallas as pl
from jax.experimental.pallas import tpu as pltpu
from jax.sharding import PartitionSpec as P


BLOCK = 128
SUB = 32
F32 = jnp.float32
BF16 = jnp.bfloat16


def split(x):
    high = x.astype(BF16)
    return high, (x - high.astype(F32)).astype(BF16)


def dot(a, b):
    return jnp.dot(a, b, preferred_element_type=F32)


def dot3(a, b):
    return dot(a[0], b[0]) + (dot(a[0], b[1]) + dot(a[1], b[0]))


def grant(mebibytes):
    return pltpu.CompilerParams(vmem_limit_bytes=mebibytes * 1024 * 1024)


def cost(flops, moved):
    return pl.CostEstimate(flops=flops, bytes_accessed=moved, transcendentals=0)


def first_kernel(width_ref, system_ref, high_ref, low_ref, inverse_ref):
    width = width_ref[pl.program_id(0)]
    order = system_ref.shape[1]
    rows = lax.broadcasted_iota(jnp.int32, (order, order), 0)
    cols = lax.broadcasted_iota(jnp.int32, (order, order), 1)
    on_diag = rows == cols
    inside = (rows < width) & (cols < width)
    system = jnp.where(inside, system_ref[0], jnp.where(on_diag, 1.0, 0.0))
    picked = jnp.where(on_diag, system, 0.0)
    start = jnp.where(on_diag, 1.0 / jnp.where(on_diag, system, 1.0), 0.0)
    down = 1.0 / jnp.sum(picked, axis=1, keepdims=True)
    across = 1.0 / jnp.sum(picked, axis=0, keepdims=True)
    inverse = 2.0 * start - down * (system * across)
    high, low = split(system)
    high_ref[0] = high
    low_ref[0] = low
    both = split(inverse)
    product = split(dot3((high, low), both))
    inverse_ref[0] = 2.0 * inverse - dot3(both, product)


def first_call(widths, systems):
    members, order, _ = systems.shape
    block = pl.BlockSpec((1, order, order), lambda s, w: (s, 0, 0))
    return pl.pallas_call(
        first_kernel,
        grid_spec=pltpu.PrefetchScalarGridSpec(
            num_scalar_prefetch=1,
            grid=(members,),
            in_specs=[block],
            out_specs=[block] * 3,
        ),
        out_shape=[
            jax.ShapeDtypeStruct(systems.shape, BF16),
            jax.ShapeDtypeStruct(systems.shape, BF16),
            jax.ShapeDtypeStruct(systems.shape, F32),
        ],
        cost_estimate=cost(12 * members * order**3, 12 * members * order**2),
        name="first_inverse",
        compiler_params=grant(20),
    )(widths, systems)


def second_kernel(width_ref, pos_ref, high_ref, low_ref, inverse_ref, upper_ref, xh_ref, xl_ref, part_ref):
    width = width_ref[pl.program_id(0)]
    order = high_ref.shape[1]
    half = upper_ref.shape[1]
    inverse = inverse_ref[0]
    both = split(inverse)
    product = split(dot3((high_ref[0], low_ref[0]), both))
    inverse = 2.0 * inverse - dot3(both, product)
    rows = lax.broadcasted_iota(jnp.int32, (order, order), 0)
    cols = lax.broadcasted_iota(jnp.int32, (order, order), 1)
    inverse = jnp.where((rows < width) & (cols < width), inverse, 0.0)
    swap = pos_ref[2] == 1
    mine = jnp.where(swap, inverse[:, half:], inverse[:, :half])
    other = jnp.where(swap, inverse[:, :half], inverse[:, half:])
    high, low = split(mine)
    upper = upper_ref[0]
    part_ref[0] = dot(high, upper) + dot(low, upper)
    high, low = split(other)
    xh_ref[0] = high
    xl_ref[0] = low


def second_call(widths, pos, high, low, inverse, upper):
    members, order, _ = high.shape
    half, cols = upper.shape[1:]
    square = pl.BlockSpec((1, order, order), lambda s, w, p: (s, 0, 0))
    tall = pl.BlockSpec((1, order, half), lambda s, w, p: (s, 0, 0))
    return pl.pallas_call(
        second_kernel,
        grid_spec=pltpu.PrefetchScalarGridSpec(
            num_scalar_prefetch=2,
            grid=(members,),
            in_specs=[square] * 3 + [pl.BlockSpec((1, half, cols), lambda s, w, p: (s, 0, 0))],
            out_specs=[tall, tall, pl.BlockSpec((1, order, cols), lambda s, w, p: (s, 0, 0))],
        ),
        out_shape=[
            jax.ShapeDtypeStruct((members, order, half), BF16),
            jax.ShapeDtypeStruct((members, order, half), BF16),
            jax.ShapeDtypeStruct((members, order, cols), F32),
        ],
        cost_estimate=cost(14 * members * order**3, 14 * members * order**2),
        name="second_inverse",
        compiler_params=grant(24),
    )(widths, pos, high, low, inverse, upper)


def scale_kernel(pos_ref, fill_ref, xh_ref, xl_ref, part_ref, upper_ref, out_ref):
    s = pl.program_id(0)
    order, cols = part_ref.shape[1:]
    pieces = order // BLOCK
    upper = upper_ref[0]
    scaled = part_ref[0] + (dot(xh_ref[0], upper) + dot(xl_ref[0], upper))
    col = pos_ref[1]
    blocks = cols // BLOCK
    parts = []
    for j in range(blocks):
        used = fill_ref[s, col * blocks + j] != 0
        tile = scaled[:, j * BLOCK : (j + 1) * BLOCK]
        parts.append(jnp.where(used, tile, jnp.zeros_like(tile)).astype(BF16))
    scaled = jnp.concatenate(parts, axis=1)
    for k in range(pieces):
        spot = lax.rem(k - col + pieces, pieces)
        out_ref[0, spot] = scaled[k * BLOCK : (k + 1) * BLOCK]


def scale_call(pos, fill, xh, xl, part, upper):
    members, order, half = xh.shape
    cols = upper.shape[2]
    pieces = order // BLOCK
    tall = pl.BlockSpec((1, order, half), lambda s, p, f: (s, 0, 0))
    return pl.pallas_call(
        scale_kernel,
        grid_spec=pltpu.PrefetchScalarGridSpec(
            num_scalar_prefetch=2,
            grid=(members,),
            in_specs=[
                tall,
                tall,
                pl.BlockSpec((1, order, cols), lambda s, p, f: (s, 0, 0)),
                pl.BlockSpec((1, half, cols), lambda s, p, f: (s, 0, 0)),
            ],
            out_specs=pl.BlockSpec((1, pieces, BLOCK, cols), lambda s, p, f: (s, 0, 0, 0)),
        ),
        out_shape=jax.ShapeDtypeStruct((members, pieces, BLOCK, cols), BF16),
        cost_estimate=cost(4 * members * order * half * cols, 8 * members * order * cols),
        name="scale_upper",
        compiler_params=grant(20),
    )(pos, fill, xh, xl, part, upper)


def update_kernel(flip, chunk, pos_ref, fill_ref, front_ref, own_ref, next_ref, far_ref, last_ref, scaled_ref, after_ref, out_ref, wide):
    members, spots, rows = own_ref.shape[0], own_ref.shape[1], own_ref.shape[3]
    side = pos_ref[0] if not flip else 1 - pos_ref[0]
    strip = 2 * rows
    base = pos_ref[2] * (spots * 2 * strip) + side * strip + chunk * rows
    pieces = (own_ref, next_ref, far_ref, last_ref)
    order = len(pieces) * BLOCK
    for s in range(members):
        for d in range(spots):
            for j in range(rows // SUB):
                spot = lax.div(base + d * 2 * strip + j * SUB, BLOCK)
                used = fill_ref[s, spot] != 0
                for k, ref in enumerate(pieces):
                    tile = ref[s, d, 0, j * SUB : (j + 1) * SUB, :]
                    begin = s * order + k * BLOCK
                    top = d * rows + j * SUB
                    wide[top : top + SUB, begin : begin + BLOCK] = jnp.where(used, tile, jnp.zeros_like(tile))
    scaled = scaled_ref[...].reshape(members * order, scaled_ref.shape[-1])
    update = dot(wide[...], scaled).reshape(spots, rows, scaled.shape[1])
    out_ref[...] = front_ref[:, 0, 0].astype(F32) - update


def update_call(flip, chunk, pos, fill, front, lowers, scaled, after):
    spots, _, _, rows, cols = front.shape
    members = scaled.shape[0]
    order = scaled.shape[1] * scaled.shape[2]

    def side(p):
        return 1 - p[0] if flip else p[0]

    piece = pl.BlockSpec((members, spots, 1, rows, BLOCK), lambda i, p, f: (0, 0, side(p), 0, 0))

    def body(*refs):
        update_kernel(flip, chunk, *refs)

    return pl.pallas_call(
        body,
        grid_spec=pltpu.PrefetchScalarGridSpec(
            num_scalar_prefetch=2,
            grid=(1,),
            in_specs=[pl.BlockSpec((spots, 1, 1, rows, cols), lambda i, p, f: (0, side(p), chunk, 0, 0))]
            + [piece] * 4
            + [pl.BlockSpec(scaled.shape, lambda i, p, f: (0, 0, 0, 0)), pl.BlockSpec(memory_space=pl.ANY)],
            out_specs=pl.BlockSpec((spots, rows, cols), lambda i, p, f: (0, 0, 0)),
            scratch_shapes=[pltpu.VMEM((spots * rows, members * order), BF16)],
        ),
        out_shape=jax.ShapeDtypeStruct((spots, rows, cols), F32),
        cost_estimate=cost(2 * spots * rows * members * order * cols, 4000000),
        compiler_params=grant(16),
    )(pos, fill, front, *lowers, scaled, after)


def round_kernel(pos_ref, kept_ref, got_ref, own_ref, *out_refs):
    place = pos_ref[3]
    own_ref[...] = kept_ref[place] + got_ref[place]
    for k, out_ref in enumerate(out_refs):
        spot = lax.bitwise_xor(place, k + 1)
        out_ref[...] = (kept_ref[spot] + got_ref[spot]).astype(out_ref.dtype)


def round_call(pos, kept, got):
    spots, rows, cols = kept.shape
    whole = pl.BlockSpec((spots, rows, cols), lambda i, p: (0, 0, 0))
    tile = pl.BlockSpec((rows, cols), lambda i, p: (0, 0))
    return pl.pallas_call(
        round_kernel,
        grid_spec=pltpu.PrefetchScalarGridSpec(
            num_scalar_prefetch=1, grid=(1,), in_specs=[whole, whole], out_specs=[tile] * spots
        ),
        out_shape=[jax.ShapeDtypeStruct((rows, cols), F32)]
        + [jax.ShapeDtypeStruct((rows, cols), F32)]
        + [jax.ShapeDtypeStruct((rows, cols), BF16)] * (spots - 2),
        cost_estimate=cost(spots * rows * cols, 10 * spots * rows * cols),
        name="round_sums",
        compiler_params=grant(12),
    )(pos, kept, got)


def final_kernel(*refs):
    out_ref = refs[-1]
    per = (len(refs) - 1) // 2
    rows = refs[0].shape[0]
    for chunk in range(2):
        group = refs[chunk * per : (chunk + 1) * per]
        total = group[0][...]
        for ref in group[1:]:
            total = total + ref[...].astype(F32)
        out_ref[0, chunk * rows : (chunk + 1) * rows] = total


def final_call(parts):
    rows, cols = parts[0].shape
    return pl.pallas_call(
        final_kernel,
        out_shape=jax.ShapeDtypeStruct((1, 2 * rows, cols), F32),
        cost_estimate=cost(len(parts) * rows * cols, 3 * len(parts) * rows * cols),
        name="final_sums",
        compiler_params=grant(8),
    )(*parts)


def on_device(front_copies, lower_panels, upper_panels, diag_blocks, block_fill, widths):
    layers, col_devices = lax.axis_size("layer"), lax.axis_size("col")
    layer = lax.axis_index("layer")
    row_index, col_index = lax.axis_index("row"), lax.axis_index("col")
    which = jnp.arange(4, dtype=jnp.int32)
    pos = jnp.where(
        which == 0,
        layer & 1,
        jnp.where(which == 1, col_index, jnp.where(which == 2, row_index, layer >> 1 & 3)),
    ).astype(jnp.int32)
    upper, fill, width_vec = upper_panels[0], block_fill[0], widths[0]
    row_count, cols = front_copies.shape[1:]
    members = upper.shape[0]
    spots = 4
    rows = row_count // (spots * 4)
    front = front_copies.reshape(spots, 2, 2, rows, cols)
    lower = lower_panels.reshape(members, spots, 2, 2, rows, BLOCK)

    def shift(block, step):
        return lax.ppermute(block, "col", [(i, (i + step) % col_devices) for i in range(col_devices)])

    def across(block, flip):
        return lax.ppermute(block, "layer", [(i, i ^ flip) for i in range(layers)])

    other_upper = lax.ppermute(upper, "row", [(0, 1), (1, 0)])
    lowers = []
    for chunk in range(2):
        own = lower[:, :, :, chunk]
        last = shift(own, 1)
        following = shift(own, -1)
        far = shift(own, 2)
        lowers.append((own, following, far, last))
    high, low, inverse = first_call(width_vec, diag_blocks[0])
    xh, xl, part = second_call(width_vec, pos, high, low, inverse, upper)
    scaled = scale_call(pos, fill, xh, xl, part, other_upper)
    finals = []
    after = scaled
    for chunk in range(2):
        sent = update_call(True, chunk, pos, fill, front, lowers[chunk], scaled, after)
        got = across(sent, 1)
        kept = update_call(False, chunk, pos, fill, front, lowers[chunk], scaled, after)
        own, one, two, three = round_call(pos, kept, got)
        after = one
        finals += [own, across(two, 4), across(three, 6), across(one, 2)]
    return final_call(finals)


def solution(mesh):
    placed = (
        P("layer", "row", "col"),
        P("layer", None, "row", "col"),
        P("layer", None, "row", "col"),
        P("layer", None, None, None),
        P("layer", None, None),
        P("layer", None),
    )

    return jax.shard_map(
        on_device, mesh=mesh, in_specs=placed, out_specs=P("layer", "row", "col"), check_vma=False
    )
```

```python
import jax
import jax.numpy as jnp
from jax import lax
from jax.experimental import pallas as pl
from jax.experimental.pallas import tpu as pltpu
from jax.sharding import PartitionSpec as P


BLOCK = 128
SUB = 32
KNEE = 32.0
STEEP = 1024.0
F32 = jnp.float32
BF16 = jnp.bfloat16
VMEM = pl.BlockSpec(memory_space=pltpu.VMEM)
SMEM = pl.BlockSpec(memory_space=pltpu.SMEM)
ANY = pl.BlockSpec(memory_space=pl.ANY)


def split(x):
    high = x.astype(BF16)
    return high, (x - high.astype(F32)).astype(BF16)


def dot(a, b):
    return jnp.dot(a, b, preferred_element_type=F32)


def dot3(a, b):
    return dot(a[0], b[0]) + (dot(a[0], b[1]) + dot(a[1], b[0]))


def code(v):
    return (v * jnp.clip(jnp.abs(v) * (1.0 / KNEE), 1.0 / STEEP, 1.0)).astype(BF16)


def decode(y):
    y = y.astype(F32)
    return y * jnp.clip(lax.rsqrt(jnp.abs(y) * (1.0 / KNEE)), 1.0, STEEP)


def grant(mebibytes):
    return pltpu.CompilerParams(vmem_limit_bytes=mebibytes * 1024 * 1024)


def cost(flops, moved):
    return pl.CostEstimate(flops=flops, bytes_accessed=moved, transcendentals=0)


def square_masks(order, width):
    rows = lax.broadcasted_iota(jnp.int32, (order, order), 0)
    cols = lax.broadcasted_iota(jnp.int32, (order, order), 1)
    return rows == cols, (rows < width) & (cols < width)


def inverse_kernel(width_ref, pos_ref, system_ref, upper_ref, xh_ref, xl_ref, part_ref):
    members, order, _ = system_ref.shape
    half = upper_ref.shape[1]
    swap = pos_ref[2] == 1
    for s in range(members):
        on_diag, inside = square_masks(order, width_ref[s])
        identity = jnp.where(on_diag, 1.0, 0.0)
        system = jnp.where(inside, system_ref[s], identity)
        picked = jnp.where(on_diag, system, 0.0)
        down = 1.0 / jnp.sum(picked, axis=1, keepdims=True)
        across = 1.0 / jnp.sum(picked, axis=0, keepdims=True)
        start = jnp.where(on_diag, down, 0.0)
        inverse = (2.0 * start - down * (system * across)).astype(BF16)
        high, low = split(system)
        residual = identity - (dot(high, inverse) + dot(low, inverse))
        inverse = inverse.astype(F32) + dot(inverse, residual.astype(BF16))
        both = split(inverse)
        residual = identity - dot3((high, low), both)
        inverse = inverse + dot3(both, split(residual))
        inverse = jnp.where(inside, inverse, 0.0)
        mine = jnp.where(swap, inverse[:, half:], inverse[:, :half])
        other = jnp.where(swap, inverse[:, :half], inverse[:, half:])
        high, low = split(mine)
        upper = upper_ref[s]
        part_ref[s] = dot(high, upper) + dot(low, upper)
        high, low = split(other)
        xh_ref[s] = high
        xl_ref[s] = low


def inverse_call(widths, pos, systems, upper):
    members, order, _ = systems.shape
    half, cols = upper.shape[1:]
    return pl.pallas_call(
        inverse_kernel,
        in_specs=[SMEM, SMEM, VMEM, VMEM],
        out_specs=[VMEM] * 3,
        out_shape=[
            jax.ShapeDtypeStruct((members, order, half), BF16),
            jax.ShapeDtypeStruct((members, order, half), BF16),
            jax.ShapeDtypeStruct((members, order, cols), F32),
        ],
        cost_estimate=cost(14 * members * order**3, 8000000),
        name="inverse",
        compiler_params=grant(20),
    )(widths, pos, systems, upper)


def scale_kernel(pos_ref, fill_ref, xh_ref, xl_ref, part_ref, upper_ref, out_ref):
    members, order, cols = part_ref.shape
    pieces = order // BLOCK
    blocks = cols // BLOCK
    col = pos_ref[1]
    for s in range(members):
        upper = upper_ref[s]
        scaled = part_ref[s] + (dot(xh_ref[s], upper) + dot(xl_ref[s], upper))
        for j in range(blocks):
            used = fill_ref[s, col * blocks + j] != 0
            lanes = slice(j * BLOCK, (j + 1) * BLOCK)
            tile = scaled[:, lanes]
            tile = jnp.where(used, tile, jnp.zeros_like(tile)).astype(BF16)
            for k in range(pieces):
                spot = lax.rem(k - col + pieces, pieces)
                out_ref[s, spot, :, lanes] = tile[k * BLOCK : (k + 1) * BLOCK]


def scale_call(pos, fill, xh, xl, part, upper):
    members, order, half = xh.shape
    cols = upper.shape[2]
    return pl.pallas_call(
        scale_kernel,
        in_specs=[SMEM, SMEM] + [VMEM] * 4,
        out_specs=VMEM,
        out_shape=jax.ShapeDtypeStruct((members, order // BLOCK, BLOCK, cols), BF16),
        cost_estimate=cost(4 * members * order * half * cols, 8 * members * order * cols),
        name="scale_upper",
        compiler_params=grant(16),
    )(pos, fill, xh, xl, part, upper)


def update_call(flip, chunk, pos, fill, front, lowers, scaled, after):
    spots, _, _, rows, cols = front.shape
    members = scaled.shape[0]
    order = scaled.shape[1] * scaled.shape[2]

    def update_kernel(pos_ref, fill_ref, front_ref, *refs):
        *piece_refs, scaled_ref, after_ref, out_ref, wide = refs
        side = 1 - pos_ref[0] if flip else pos_ref[0]
        strip = 2 * rows
        base = pos_ref[2] * (spots * 2 * strip) + side * strip + chunk * rows
        for s in range(members):
            for d in range(spots):
                for j in range(rows // SUB):
                    spot = lax.div(base + d * 2 * strip + j * SUB, BLOCK)
                    used = fill_ref[s, spot] != 0
                    for k, ref in enumerate(piece_refs):
                        tile = ref[s, d, side, j * SUB : (j + 1) * SUB, :]
                        begin = s * order + k * BLOCK
                        top = d * rows + j * SUB
                        wide[top : top + SUB, begin : begin + BLOCK] = jnp.where(used, tile, jnp.zeros_like(tile))
        flat = scaled_ref[...].reshape(members * order, cols)
        update = dot(wide[...], flat).reshape(spots, rows, cols)
        for d in range(spots):
            out_ref[d] = front_ref[d, side, chunk].astype(F32) - update[d]

    return pl.pallas_call(
        update_kernel,
        in_specs=[SMEM, SMEM] + [VMEM] * 6 + [ANY],
        out_specs=VMEM,
        scratch_shapes=[pltpu.VMEM((spots * rows, members * order), BF16)],
        out_shape=jax.ShapeDtypeStruct((spots, rows, cols), F32),
        cost_estimate=cost(2 * spots * rows * members * order * cols, 4000000),
        compiler_params=grant(12),
    )(pos, fill, front, *lowers, scaled, after)


def round_kernel(pos_ref, kept_ref, got_ref, own_ref, *out_refs):
    place = pos_ref[3]
    for k, out_ref in enumerate(out_refs):
        spot = lax.bitwise_xor(place, k + 1)
        out_ref[...] = code(kept_ref[spot] + got_ref[spot])
    own_ref[...] = kept_ref[place] + got_ref[place]


def round_call(pos, kept, got):
    spots, rows, cols = kept.shape
    return pl.pallas_call(
        round_kernel,
        in_specs=[SMEM, VMEM, VMEM],
        out_specs=[VMEM] * spots,
        out_shape=[jax.ShapeDtypeStruct((rows, cols), F32)]
        + [jax.ShapeDtypeStruct((rows, cols), BF16)] * (spots - 1),
        cost_estimate=cost(spots * rows * cols, 10 * spots * rows * cols),
        name="round_sums",
        compiler_params=grant(8),
    )(pos, kept, got)


def final_kernel(*refs):
    out_ref = refs[-1]
    per = (len(refs) - 1) // 2
    rows = refs[0].shape[0]
    for chunk in range(2):
        group = refs[chunk * per : (chunk + 1) * per]
        total = group[0][...]
        for ref in group[1:]:
            total = total + decode(ref[...])
        out_ref[0, chunk * rows : (chunk + 1) * rows] = total


def final_call(parts):
    rows, cols = parts[0].shape
    return pl.pallas_call(
        final_kernel,
        in_specs=[VMEM] * len(parts),
        out_specs=VMEM,
        out_shape=jax.ShapeDtypeStruct((1, 2 * rows, cols), F32),
        cost_estimate=cost(len(parts) * rows * cols, 3 * len(parts) * rows * cols),
        name="final_sums",
        compiler_params=grant(8),
    )(*parts)


def on_device(front_copies, lower_panels, upper_panels, diag_blocks, block_fill, widths):
    layers, col_devices = lax.axis_size("layer"), lax.axis_size("col")
    layer = lax.axis_index("layer")
    row_index, col_index = lax.axis_index("row"), lax.axis_index("col")
    which = jnp.arange(4, dtype=jnp.int32)
    pos = jnp.where(
        which == 0,
        layer & 1,
        jnp.where(which == 1, col_index, jnp.where(which == 2, row_index, layer >> 1 & 3)),
    ).astype(jnp.int32)
    upper, fill, width_vec = upper_panels[0], block_fill[0], widths[0]
    row_count, cols = front_copies.shape[1:]
    members = upper.shape[0]
    spots = 4
    rows = row_count // (spots * 4)
    front = front_copies.reshape(spots, 2, 2, rows, cols)
    lower = lower_panels.reshape(members, spots, 2, 2, rows, BLOCK)

    def shift(block, step):
        return lax.ppermute(block, "col", [(i, (i + step) % col_devices) for i in range(col_devices)])

    def across(block, flip):
        return lax.ppermute(block, "layer", [(i, i ^ flip) for i in range(layers)])

    other_upper = lax.ppermute(upper, "row", [(0, 1), (1, 0)])
    lowers = []
    for chunk in range(2):
        own = lower[:, :, :, chunk]
        last = shift(own, 1)
        following = shift(own, -1)
        far = shift(own, 2)
        lowers.append((own, following, far, last))
    xh, xl, part = inverse_call(width_vec, pos, diag_blocks[0], upper)
    scaled = scale_call(pos, fill, xh, xl, part, other_upper)
    finals = []
    after = scaled
    for chunk in range(2):
        sent = update_call(True, chunk, pos, fill, front, lowers[chunk], scaled, after)
        got = across(sent, 1)
        kept = update_call(False, chunk, pos, fill, front, lowers[chunk], scaled, after)
        own, one, two, three = round_call(pos, kept, got)
        after = one
        finals += [own, across(two, 4), across(three, 6), across(one, 2)]
    return final_call(finals)


def solution(mesh):
    placed = (
        P("layer", "row", "col"),
        P("layer", None, "row", "col"),
        P("layer", None, "row", "col"),
        P("layer", None, None, None),
        P("layer", None, None),
        P("layer", None),
    )

    return jax.shard_map(
        on_device, mesh=mesh, in_specs=placed, out_specs=P("layer", "row", "col"), check_vma=False
    )
```

```python
import jax
import jax.numpy as jnp
from jax import lax
from jax.experimental import pallas as pl
from jax.experimental.pallas import tpu as pltpu
from jax.sharding import PartitionSpec as P


BLOCK = 128
SUB = 32
KNEE = 32.0
STEEP = 1024.0
F32 = jnp.float32
BF16 = jnp.bfloat16
VMEM = pl.BlockSpec(memory_space=pltpu.VMEM)
SMEM = pl.BlockSpec(memory_space=pltpu.SMEM)
ANY = pl.BlockSpec(memory_space=pl.ANY)


def split(x):
    high = x.astype(BF16)
    return high, (x - high.astype(F32)).astype(BF16)


def dot(a, b):
    return jnp.dot(a, b, preferred_element_type=F32)


def dot3(a, b):
    return dot(a[0], b[0]) + (dot(a[0], b[1]) + dot(a[1], b[0]))


def code(v):
    return (v * jnp.clip(jnp.abs(v) * (1.0 / KNEE), 1.0 / STEEP, 1.0)).astype(BF16)


def decode(y):
    y = y.astype(F32)
    return y * jnp.clip(lax.rsqrt(jnp.abs(y) * (1.0 / KNEE)), 1.0, STEEP)


def grant(mebibytes):
    return pltpu.CompilerParams(vmem_limit_bytes=mebibytes * 1024 * 1024)


def cost(flops, moved):
    return pl.CostEstimate(flops=flops, bytes_accessed=moved, transcendentals=0)


def square_masks(order, width):
    rows = lax.broadcasted_iota(jnp.int32, (order, order), 0)
    cols = lax.broadcasted_iota(jnp.int32, (order, order), 1)
    return rows == cols, (rows < width) & (cols < width)


def place_kernel(in_ref, out_ref):
    for k in range(in_ref.shape[0]):
        out_ref[k] = in_ref[k]


def place_call(pos):
    return pl.pallas_call(
        place_kernel,
        in_specs=[SMEM],
        out_specs=SMEM,
        out_shape=jax.ShapeDtypeStruct(pos.shape, pos.dtype),
        cost_estimate=cost(10**10, 10**7),
        name="place",
        compiler_params=grant(1),
    )(pos)


def inverse_call(s, widths, pos, systems, upper):
    order = systems.shape[1]
    half, cols = upper.shape[1:]

    def inverse_kernel(width_ref, pos_ref, system_ref, upper_ref, xh_ref, xl_ref, part_ref):
        swap = pos_ref[2] == 1
        on_diag, inside = square_masks(order, width_ref[s])
        identity = jnp.where(on_diag, 1.0, 0.0)
        system = jnp.where(inside, system_ref[s], identity)
        picked = jnp.where(on_diag, system, 0.0)
        down = 1.0 / jnp.sum(picked, axis=1, keepdims=True)
        across = 1.0 / jnp.sum(picked, axis=0, keepdims=True)
        start = jnp.where(on_diag, down, 0.0)
        inverse = (2.0 * start - down * (system * across)).astype(BF16)
        high, low = split(system)
        residual = identity - (dot(high, inverse) + dot(low, inverse))
        inverse = inverse.astype(F32) + dot(inverse, residual.astype(BF16))
        both = split(inverse)
        residual = identity - dot3((high, low), both)
        inverse = inverse + dot3(both, split(residual))
        inverse = jnp.where(inside, inverse, 0.0)
        mine = jnp.where(swap, inverse[:, half:], inverse[:, :half])
        other = jnp.where(swap, inverse[:, :half], inverse[:, half:])
        high, low = split(mine)
        part_ref[...] = dot(high, upper_ref[s]) + dot(low, upper_ref[s])
        high, low = split(other)
        xh_ref[...] = high
        xl_ref[...] = low

    return pl.pallas_call(
        inverse_kernel,
        in_specs=[SMEM, SMEM, VMEM, VMEM],
        out_specs=[VMEM] * 3,
        out_shape=[
            jax.ShapeDtypeStruct((order, half), BF16),
            jax.ShapeDtypeStruct((order, half), BF16),
            jax.ShapeDtypeStruct((order, cols), F32),
        ],
        cost_estimate=cost(20 * order**3, 4000000),
        compiler_params=grant(16),
    )(widths, pos, systems, upper)


def scale_call(pos, fill, inverses, upper):
    members, half, cols = upper.shape
    order = inverses[0][0].shape[0]

    def scale_kernel(pos_ref, fill_ref, *refs):
        *inverse_refs, upper_ref, out_ref = refs
        pieces = order // BLOCK
        blocks = cols // BLOCK
        col = pos_ref[1]
        for s in range(members):
            xh_ref, xl_ref, part_ref = inverse_refs[3 * s : 3 * s + 3]
            upper = upper_ref[s]
            scaled = part_ref[...] + (dot(xh_ref[...], upper) + dot(xl_ref[...], upper))
            for j in range(blocks):
                used = fill_ref[s, col * blocks + j] != 0
                lanes = slice(j * BLOCK, (j + 1) * BLOCK)
                tile = scaled[:, lanes]
                tile = jnp.where(used, tile, jnp.zeros_like(tile)).astype(BF16)
                for k in range(pieces):
                    spot = lax.rem(k - col + pieces, pieces)
                    out_ref[s, spot, :, lanes] = tile[k * BLOCK : (k + 1) * BLOCK]

    flat = [x for inverse in inverses for x in inverse]
    return pl.pallas_call(
        scale_kernel,
        in_specs=[SMEM, SMEM] + [VMEM] * (len(flat) + 1),
        out_specs=VMEM,
        out_shape=jax.ShapeDtypeStruct((members, order // BLOCK, BLOCK, cols), BF16),
        cost_estimate=cost(4 * members * order * half * cols, 8 * members * order * cols),
        name="scale_upper",
        compiler_params=grant(16),
    )(pos, fill, *flat, upper)


def update_call(flip, chunk, pos, fill, front, lowers, scaled, after):
    spots, _, _, rows, cols = front.shape
    members = scaled.shape[0]
    order = scaled.shape[1] * scaled.shape[2]

    def update_kernel(pos_ref, fill_ref, front_ref, *refs):
        own_ref, next_ref, far_refs, last_ref = refs[0], refs[1], refs[2:4], refs[4]
        scaled_ref, _, out_ref, wide = refs[5:]
        side = 1 - pos_ref[0] if flip else pos_ref[0]
        strip = 2 * rows
        base = pos_ref[2] * (spots * 2 * strip) + side * strip + chunk * rows
        for s in range(members):
            for d in range(spots):
                for j in range(rows // SUB):
                    spot = lax.div(base + d * 2 * strip + j * SUB, BLOCK)
                    used = fill_ref[s, spot] != 0
                    spans = (d, side, slice(j * SUB, (j + 1) * SUB))
                    tiles = (own_ref[s, *spans], next_ref[s, *spans], far_refs[s][*spans], last_ref[s, *spans])
                    for k, tile in enumerate(tiles):
                        begin = s * order + k * BLOCK
                        top = d * rows + j * SUB
                        wide[top : top + SUB, begin : begin + BLOCK] = jnp.where(used, tile, jnp.zeros_like(tile))
        flat = scaled_ref[...].reshape(members * order, cols)
        update = dot(wide[...], flat).reshape(spots, rows, cols)
        for d in range(spots):
            out_ref[d] = front_ref[d, side, chunk].astype(F32) - update[d]

    return pl.pallas_call(
        update_kernel,
        in_specs=[SMEM, SMEM] + [VMEM] * 7 + [ANY],
        out_specs=VMEM,
        scratch_shapes=[pltpu.VMEM((spots * rows, members * order), BF16)],
        out_shape=jax.ShapeDtypeStruct((spots, rows, cols), F32),
        cost_estimate=cost(2 * spots * rows * members * order * cols, 4000000),
        compiler_params=grant(12),
    )(pos, fill, front, *lowers, scaled, after)


def pair_kernel(pos_ref, kept_ref, got_ref, own_ref, out_ref):
    parity = pos_ref[3] & 1
    for j in range(own_ref.shape[0]):
        spot = 2 * j + 1 - parity
        out_ref[j] = code(kept_ref[spot] + got_ref[spot])
    for j in range(own_ref.shape[0]):
        spot = 2 * j + parity
        own_ref[j] = kept_ref[spot] + got_ref[spot]


def pair_call(pos, kept, got):
    spots, rows, cols = kept.shape
    half = (spots // 2, rows, cols)
    return pl.pallas_call(
        pair_kernel,
        in_specs=[SMEM, VMEM, VMEM],
        out_specs=[VMEM] * 2,
        out_shape=[jax.ShapeDtypeStruct(half, F32), jax.ShapeDtypeStruct(half, BF16)],
        cost_estimate=cost(spots * rows * cols, 10 * spots * rows * cols),
        compiler_params=grant(8),
    )(pos, kept, got)


def quarter_kernel(pos_ref, own_ref, got_ref, part_ref, out_ref):
    place = pos_ref[3] >> 1
    out_ref[...] = code(own_ref[1 - place] + decode(got_ref[1 - place]))
    part_ref[...] = own_ref[place] + decode(got_ref[place])


def quarter_call(pos, own, got):
    _, rows, cols = own.shape
    return pl.pallas_call(
        quarter_kernel,
        in_specs=[SMEM, VMEM, VMEM],
        out_specs=[VMEM] * 2,
        out_shape=[jax.ShapeDtypeStruct((rows, cols), F32), jax.ShapeDtypeStruct((rows, cols), BF16)],
        cost_estimate=cost(8 * rows * cols, 16 * rows * cols),
        compiler_params=grant(8),
    )(pos, own, got)


def final_kernel(*refs):
    *in_refs, out_ref = refs
    rows = in_refs[0].shape[0]
    for chunk in range(len(in_refs) // 2):
        part_ref, got_ref = in_refs[2 * chunk : 2 * chunk + 2]
        out_ref[0, chunk * rows : (chunk + 1) * rows] = part_ref[...] + decode(got_ref[...])


def final_call(parts):
    rows, cols = parts[0].shape
    return pl.pallas_call(
        final_kernel,
        in_specs=[VMEM] * len(parts),
        out_specs=VMEM,
        out_shape=jax.ShapeDtypeStruct((1, len(parts) // 2 * rows, cols), F32),
        cost_estimate=cost(len(parts) * rows * cols, 3 * len(parts) * rows * cols),
        name="final_sums",
        compiler_params=grant(8),
    )(*parts)


def on_device(front_copies, lower_panels, upper_panels, diag_blocks, block_fill, widths):
    layers, col_devices = lax.axis_size("layer"), lax.axis_size("col")
    layer = lax.axis_index("layer")
    row_index, col_index = lax.axis_index("row"), lax.axis_index("col")
    which = jnp.arange(4, dtype=jnp.int32)
    pos = jnp.where(
        which == 0,
        layer & 1,
        jnp.where(which == 1, col_index, jnp.where(which == 2, row_index, layer >> 1 & 3)),
    ).astype(jnp.int32)
    pos = place_call(pos)
    upper, fill, width_vec = upper_panels[0], block_fill[0], widths[0]
    row_count, cols = front_copies.shape[1:]
    members = upper.shape[0]
    spots = 4
    rows = row_count // (spots * 4)
    front = front_copies.reshape(spots, 2, 2, rows, cols)
    lower = lower_panels.reshape(members, spots, 2, 2, rows, BLOCK)

    def shift(block, step):
        return lax.ppermute(block, "col", [(i, (i + step) % col_devices) for i in range(col_devices)])

    def across(block, flip):
        return lax.ppermute(block, "layer", [(i, i ^ flip) for i in range(layers)])

    other_upper = lax.ppermute(upper, "row", [(0, 1), (1, 0)])
    near = []
    for chunk in range(2):
        own = lower[:, :, :, chunk]
        near.append((own, shift(own, -1), shift(own, 1)))
    inverses = [inverse_call(s, width_vec, pos, diag_blocks[0], upper) for s in range(members)]
    scaled = scale_call(pos, fill, inverses, other_upper)
    parts = []
    after = scaled
    for chunk in range(2):
        own, following, last = near[chunk]
        far = (shift(last[0], 1), shift(following[1], -1))
        lowers = (own, following, *far, last)
        sent = update_call(True, chunk, pos, fill, front, lowers, scaled, after)
        got = across(sent, 1)
        kept = update_call(False, chunk, pos, fill, front, lowers, scaled, after)
        pair, after = pair_call(pos, kept, got)
        got = across(after, 2)
        part, quarter = quarter_call(pos, pair, got)
        parts += [part, across(quarter, 4)]
    return final_call(parts)


def solution(mesh):
    placed = (
        P("layer", "row", "col"),
        P("layer", None, "row", "col"),
        P("layer", None, "row", "col"),
        P("layer", None, None, None),
        P("layer", None, None),
        P("layer", None),
    )

    return jax.shard_map(on_device, mesh=mesh, in_specs=placed, out_specs=P("layer", "row", "col"), check_vma=False)
```

```python
import jax
import jax.numpy as jnp
from jax import lax
from jax.experimental import pallas as pl
from jax.experimental.pallas import tpu as pltpu
from jax.sharding import PartitionSpec as P


BLOCK = 128
SUB = 32
KNEE = 32.0
STEEP = 1024.0
F32 = jnp.float32
BF16 = jnp.bfloat16
VMEM = pl.BlockSpec(memory_space=pltpu.VMEM)
SMEM = pl.BlockSpec(memory_space=pltpu.SMEM)
ANY = pl.BlockSpec(memory_space=pl.ANY)


def split(x):
    high = x.astype(BF16)
    return high, (x - high.astype(F32)).astype(BF16)


def dot(a, b):
    return jnp.dot(a, b, preferred_element_type=F32)


def dot3(a, b):
    return dot(a[0], b[0]) + (dot(a[0], b[1]) + dot(a[1], b[0]))


def code(v):
    return (v * jnp.clip(jnp.abs(v) * (1.0 / KNEE), 1.0 / STEEP, 1.0)).astype(BF16)


def decode(y):
    y = y.astype(F32)
    return y * jnp.clip(lax.rsqrt(jnp.abs(y) * (1.0 / KNEE)), 1.0, STEEP)


def grant(mebibytes):
    return pltpu.CompilerParams(vmem_limit_bytes=mebibytes * 1024 * 1024)


def cost(flops, moved):
    return pl.CostEstimate(flops=flops, bytes_accessed=moved, transcendentals=0)


def square_masks(order, width):
    rows = lax.broadcasted_iota(jnp.int32, (order, order), 0)
    cols = lax.broadcasted_iota(jnp.int32, (order, order), 1)
    return rows == cols, (rows < width) & (cols < width)


def place_kernel(in_ref, out_ref):
    for k in range(in_ref.shape[0]):
        out_ref[k] = in_ref[k]


def place_call(pos):
    return pl.pallas_call(
        place_kernel,
        in_specs=[SMEM],
        out_specs=SMEM,
        out_shape=jax.ShapeDtypeStruct(pos.shape, pos.dtype),
        cost_estimate=cost(10**10, 10**7),
        name="place",
        compiler_params=grant(1),
    )(pos)


def inverse_kernel(width_ref, pos_ref, system_ref, upper_ref, xh_ref, xl_ref, part_ref):
    members, order, _ = system_ref.shape
    half = upper_ref.shape[1]
    swap = pos_ref[2] == 1
    for s in range(members):
        on_diag, inside = square_masks(order, width_ref[s])
        identity = jnp.where(on_diag, 1.0, 0.0)
        system = jnp.where(inside, system_ref[s], identity)
        picked = jnp.where(on_diag, system, 0.0)
        down = 1.0 / jnp.sum(picked, axis=1, keepdims=True)
        across = 1.0 / jnp.sum(picked, axis=0, keepdims=True)
        start = jnp.where(on_diag, down, 0.0)
        inverse = (2.0 * start - down * (system * across)).astype(BF16)
        high, low = split(system)
        residual = identity - (dot(high, inverse) + dot(low, inverse))
        inverse = inverse.astype(F32) + dot(inverse, residual.astype(BF16))
        both = split(inverse)
        residual = identity - dot3((high, low), both)
        inverse = inverse + dot3(both, split(residual))
        inverse = jnp.where(inside, inverse, 0.0)
        mine = jnp.where(swap, inverse[:, half:], inverse[:, :half])
        other = jnp.where(swap, inverse[:, :half], inverse[:, half:])
        high, low = split(mine)
        upper = upper_ref[s]
        part_ref[s] = dot(high, upper) + dot(low, upper)
        high, low = split(other)
        xh_ref[s] = high
        xl_ref[s] = low


def inverse_call(widths, pos, systems, upper):
    members, order, _ = systems.shape
    half, cols = upper.shape[1:]
    return pl.pallas_call(
        inverse_kernel,
        in_specs=[SMEM, SMEM, VMEM, VMEM],
        out_specs=[VMEM] * 3,
        out_shape=[
            jax.ShapeDtypeStruct((members, order, half), BF16),
            jax.ShapeDtypeStruct((members, order, half), BF16),
            jax.ShapeDtypeStruct((members, order, cols), F32),
        ],
        cost_estimate=cost(14 * members * order**3, 8000000),
        name="inverse",
        compiler_params=grant(20),
    )(widths, pos, systems, upper)


def scale_kernel(pos_ref, fill_ref, xh_ref, xl_ref, part_ref, upper_ref, out_ref):
    members, order, cols = part_ref.shape
    pieces = order // BLOCK
    blocks = cols // BLOCK
    col = pos_ref[1]
    for s in range(members):
        upper = upper_ref[s]
        scaled = part_ref[s] + (dot(xh_ref[s], upper) + dot(xl_ref[s], upper))
        for j in range(blocks):
            used = fill_ref[s, col * blocks + j] != 0
            lanes = slice(j * BLOCK, (j + 1) * BLOCK)
            tile = scaled[:, lanes]
            tile = jnp.where(used, tile, jnp.zeros_like(tile)).astype(BF16)
            for k in range(pieces):
                spot = lax.rem(k - col + pieces, pieces)
                out_ref[s, spot, :, lanes] = tile[k * BLOCK : (k + 1) * BLOCK]


def scale_call(pos, fill, xh, xl, part, upper):
    members, order, half = xh.shape
    cols = upper.shape[2]
    return pl.pallas_call(
        scale_kernel,
        in_specs=[SMEM, SMEM] + [VMEM] * 4,
        out_specs=VMEM,
        out_shape=jax.ShapeDtypeStruct((members, order // BLOCK, BLOCK, cols), BF16),
        cost_estimate=cost(4 * members * order * half * cols, 8 * members * order * cols),
        name="scale_upper",
        compiler_params=grant(16),
    )(pos, fill, xh, xl, part, upper)


def update_call(flip, chunk, pos, fill, front, lowers, scaled, after):
    spots, _, _, rows, cols = front.shape
    members = scaled.shape[0]
    order = scaled.shape[1] * scaled.shape[2]

    def update_kernel(pos_ref, fill_ref, front_ref, *refs):
        own_ref, next_ref, last_ref, *far_refs, scaled_ref, _, out_ref, wide = refs
        if len(far_refs) == 1:
            far_refs = [far_refs[0].at[s] for s in range(members)]
        side = 1 - pos_ref[0] if flip else pos_ref[0]
        strip = 2 * rows
        base = pos_ref[2] * (spots * 2 * strip) + side * strip + chunk * rows
        for s in range(members):
            for d in range(spots):
                for j in range(rows // SUB):
                    spot = lax.div(base + d * 2 * strip + j * SUB, BLOCK)
                    used = fill_ref[s, spot] != 0
                    spans = (d, side, slice(j * SUB, (j + 1) * SUB))
                    tiles = (own_ref[s, *spans], next_ref[s, *spans], far_refs[s][*spans], last_ref[s, *spans])
                    for k, tile in enumerate(tiles):
                        begin = s * order + k * BLOCK
                        top = d * rows + j * SUB
                        wide[top : top + SUB, begin : begin + BLOCK] = jnp.where(used, tile, jnp.zeros_like(tile))
        flat = scaled_ref[...].reshape(members * order, cols)
        update = dot(wide[...], flat).reshape(spots, rows, cols)
        for d in range(spots):
            copy = front_ref[d, side, chunk].astype(F32) - update[d]
            out_ref[d] = code(copy) if flip else copy

    return pl.pallas_call(
        update_kernel,
        in_specs=[SMEM, SMEM] + [VMEM] * (len(lowers) + 2) + [ANY],
        out_specs=VMEM,
        scratch_shapes=[pltpu.VMEM((spots * rows, members * order), BF16)],
        out_shape=jax.ShapeDtypeStruct((spots, rows, cols), BF16 if flip else F32),
        cost_estimate=cost(2 * spots * rows * members * order * cols, 4000000),
        compiler_params=grant(12),
    )(pos, fill, front, *lowers, scaled, after)


def round_kernel(pos_ref, kept_ref, got_ref, own_ref, *out_refs):
    place = pos_ref[3]
    for k, out_ref in enumerate(out_refs):
        spot = lax.bitwise_xor(place, k + 1)
        out_ref[...] = code(kept_ref[spot] + decode(got_ref[spot]))
    own_ref[...] = kept_ref[place] + decode(got_ref[place])


def round_call(pos, kept, got):
    spots, rows, cols = kept.shape
    return pl.pallas_call(
        round_kernel,
        in_specs=[SMEM, VMEM, VMEM],
        out_specs=[VMEM] * spots,
        out_shape=[jax.ShapeDtypeStruct((rows, cols), F32)]
        + [jax.ShapeDtypeStruct((rows, cols), BF16)] * (spots - 1),
        cost_estimate=cost(spots * rows * cols, 10 * spots * rows * cols),
        compiler_params=grant(8),
    )(pos, kept, got)


def final_kernel(*refs):
    out_ref = refs[-1]
    per = (len(refs) - 1) // 2
    rows = refs[0].shape[0]
    for chunk in range(2):
        group = refs[chunk * per : (chunk + 1) * per]
        total = group[0][...]
        for ref in group[1:]:
            total = total + decode(ref[...])
        out_ref[0, chunk * rows : (chunk + 1) * rows] = total


def final_call(parts):
    rows, cols = parts[0].shape
    return pl.pallas_call(
        final_kernel,
        in_specs=[VMEM] * len(parts),
        out_specs=VMEM,
        out_shape=jax.ShapeDtypeStruct((1, 2 * rows, cols), F32),
        cost_estimate=cost(len(parts) * rows * cols, 3 * len(parts) * rows * cols),
        name="final_sums",
        compiler_params=grant(8),
    )(*parts)


def on_device(front_copies, lower_panels, upper_panels, diag_blocks, block_fill, widths):
    layers, col_devices = lax.axis_size("layer"), lax.axis_size("col")
    layer = lax.axis_index("layer")
    row_index, col_index = lax.axis_index("row"), lax.axis_index("col")
    which = jnp.arange(4, dtype=jnp.int32)
    pos = jnp.where(
        which == 0,
        layer & 1,
        jnp.where(which == 1, col_index, jnp.where(which == 2, row_index, layer >> 1 & 3)),
    ).astype(jnp.int32)
    pos = place_call(pos)
    upper, fill, width_vec = upper_panels[0], block_fill[0], widths[0]
    row_count, cols = front_copies.shape[1:]
    members = upper.shape[0]
    spots = 4
    rows = row_count // (spots * 4)
    front = front_copies.reshape(spots, 2, 2, rows, cols)
    lower = lower_panels.reshape(members, spots, 2, 2, rows, BLOCK)

    def shift(block, step):
        return lax.ppermute(block, "col", [(i, (i + step) % col_devices) for i in range(col_devices)])

    def across(block, flip):
        return lax.ppermute(block, "layer", [(i, i ^ flip) for i in range(layers)])

    other_upper = lax.ppermute(upper, "row", [(0, 1), (1, 0)])
    lowers = []
    for chunk in range(2):
        own = lower[:, :, :, chunk]
        following, last = shift(own, -1), shift(own, 1)
        if chunk == 0:
            far = (shift(own, 2),)
        else:
            far = (shift(last[0], 1), shift(following[1], -1))
        lowers.append((own, following, last, *far))
    xh, xl, part = inverse_call(width_vec, pos, diag_blocks[0], upper)
    scaled = scale_call(pos, fill, xh, xl, part, other_upper)
    finals = []
    after = scaled
    for chunk in range(2):
        sent = update_call(True, chunk, pos, fill, front, lowers[chunk], scaled, after)
        got = across(sent, 1)
        kept = update_call(False, chunk, pos, fill, front, lowers[chunk], scaled, after)
        own, one, two, three = round_call(pos, kept, got)
        after = one
        finals += [own, across(two, 4), across(three, 6), across(one, 2)]
    return final_call(finals)


def solution(mesh):
    placed = (
        P("layer", "row", "col"),
        P("layer", None, "row", "col"),
        P("layer", None, "row", "col"),
        P("layer", None, None, None),
        P("layer", None, None),
        P("layer", None),
    )

    return jax.shard_map(
        on_device, mesh=mesh, in_specs=placed, out_specs=P("layer", "row", "col"), check_vma=False
    )
```

```python
import jax
import jax.numpy as jnp
from jax import lax
from jax.experimental import pallas as pl
from jax.experimental.pallas import tpu as pltpu
from jax.sharding import PartitionSpec as P


BLOCK = 128
SUB = 32
KNEE = 32.0
STEEP = 1024.0
F32 = jnp.float32
BF16 = jnp.bfloat16
VMEM = pl.BlockSpec(memory_space=pltpu.VMEM)
SMEM = pl.BlockSpec(memory_space=pltpu.SMEM)
ANY = pl.BlockSpec(memory_space=pl.ANY)


def split(x):
    high = x.astype(BF16)
    return high, (x - high.astype(F32)).astype(BF16)


def dot(a, b):
    return jnp.dot(a, b, preferred_element_type=F32)


def dot3(a, b):
    return dot(a[0], b[0]) + (dot(a[0], b[1]) + dot(a[1], b[0]))


def code(v):
    return (v * jnp.clip(jnp.abs(v) * (1.0 / KNEE), 1.0 / STEEP, 1.0)).astype(BF16)


def decode(y):
    y = y.astype(F32)
    return y * jnp.clip(lax.rsqrt(jnp.abs(y) * (1.0 / KNEE)), 1.0, STEEP)


def grant(mebibytes):
    return pltpu.CompilerParams(vmem_limit_bytes=mebibytes * 1024 * 1024)


def cost(flops, moved):
    return pl.CostEstimate(flops=flops, bytes_accessed=moved, transcendentals=0)


def square_masks(order, width):
    rows = lax.broadcasted_iota(jnp.int32, (order, order), 0)
    cols = lax.broadcasted_iota(jnp.int32, (order, order), 1)
    return rows == cols, (rows < width) & (cols < width)


def mark_kernel(in_ref, out_ref):
    for k in range(in_ref.shape[0]):
        out_ref[k] = in_ref[k]


def mark_call(pos):
    return pl.pallas_call(
        mark_kernel,
        in_specs=[SMEM],
        out_specs=SMEM,
        out_shape=jax.ShapeDtypeStruct(pos.shape, pos.dtype),
        cost_estimate=cost(10**10, 10**7),
        name="mark",
        compiler_params=grant(1),
    )(pos)


def inverse_kernel(width_ref, pos_ref, system_ref, upper_ref, xh_ref, xl_ref, part_ref):
    members, order, _ = system_ref.shape
    half = upper_ref.shape[1]
    swap = pos_ref[2] == 1
    for s in range(members):
        on_diag, inside = square_masks(order, width_ref[s])
        identity = jnp.where(on_diag, 1.0, 0.0)
        system = jnp.where(inside, system_ref[s], identity)
        picked = jnp.where(on_diag, system, 0.0)
        down = 1.0 / jnp.sum(picked, axis=1, keepdims=True)
        across = 1.0 / jnp.sum(picked, axis=0, keepdims=True)
        start = jnp.where(on_diag, down, 0.0)
        inverse = (2.0 * start - down * (system * across)).astype(BF16)
        high, low = split(system)
        residual = identity - (dot(high, inverse) + dot(low, inverse))
        inverse = inverse.astype(F32) + dot(inverse, residual.astype(BF16))
        both = split(inverse)
        residual = identity - dot3((high, low), both)
        inverse = inverse + dot3(both, split(residual))
        inverse = jnp.where(inside, inverse, 0.0)
        mine = jnp.where(swap, inverse[:, half:], inverse[:, :half])
        other = jnp.where(swap, inverse[:, :half], inverse[:, half:])
        high, low = split(mine)
        upper = upper_ref[s]
        part_ref[s] = dot(high, upper) + dot(low, upper)
        high, low = split(other)
        xh_ref[s] = high
        xl_ref[s] = low


def inverse_call(widths, pos, systems, upper):
    members, order, _ = systems.shape
    half, cols = upper.shape[1:]
    return pl.pallas_call(
        inverse_kernel,
        in_specs=[SMEM, SMEM, VMEM, VMEM],
        out_specs=[VMEM] * 3,
        out_shape=[
            jax.ShapeDtypeStruct((members, order, half), BF16),
            jax.ShapeDtypeStruct((members, order, half), BF16),
            jax.ShapeDtypeStruct((members, order, cols), F32),
        ],
        cost_estimate=cost(14 * members * order**3, 8000000),
        name="inverse",
        compiler_params=grant(20),
    )(widths, pos, systems, upper)


def pick_kernel(last_ref, following_ref, *out_refs):
    for chunk in range(2):
        out_refs[2 * chunk][...] = last_ref[0, :, :, chunk]
        out_refs[2 * chunk + 1][...] = following_ref[1, :, :, chunk]


def pick_call(last, following):
    _, spots, sides, _, rows, depth = last.shape
    shape = jax.ShapeDtypeStruct((spots, sides, rows, depth), BF16)
    return pl.pallas_call(
        pick_kernel,
        in_specs=[VMEM] * 2,
        out_specs=[VMEM] * 4,
        out_shape=[shape] * 4,
        cost_estimate=cost(1000, 4000000),
        name="pick",
        compiler_params=grant(4),
    )(last, following)


def scale_kernel(pos_ref, fill_ref, xh_ref, xl_ref, part_ref, upper_ref, out_ref):
    members, order, cols = part_ref.shape
    pieces = order // BLOCK
    blocks = cols // BLOCK
    col = pos_ref[1]
    for s in range(members):
        upper = upper_ref[s]
        scaled = part_ref[s] + (dot(xh_ref[s], upper) + dot(xl_ref[s], upper))
        for j in range(blocks):
            used = fill_ref[s, col * blocks + j] != 0
            lanes = slice(j * BLOCK, (j + 1) * BLOCK)
            tile = scaled[:, lanes]
            tile = jnp.where(used, tile, jnp.zeros_like(tile)).astype(BF16)
            for k in range(pieces):
                spot = lax.rem(k - col + pieces, pieces)
                out_ref[s, spot, :, lanes] = tile[k * BLOCK : (k + 1) * BLOCK]


def scale_call(pos, fill, xh, xl, part, upper):
    members, order, half = xh.shape
    cols = upper.shape[2]
    return pl.pallas_call(
        scale_kernel,
        in_specs=[SMEM, SMEM] + [VMEM] * 4,
        out_specs=VMEM,
        out_shape=jax.ShapeDtypeStruct((members, order // BLOCK, BLOCK, cols), BF16),
        cost_estimate=cost(4 * members * order * half * cols, 8 * members * order * cols),
        name="scale_upper",
        compiler_params=grant(16),
    )(pos, fill, xh, xl, part, upper)


def update_call(flip, chunk, pos, fill, front, lowers, scaled, after):
    spots, _, _, rows, cols = front.shape
    members = scaled.shape[0]
    order = scaled.shape[1] * scaled.shape[2]

    def update_kernel(pos_ref, fill_ref, front_ref, *refs):
        own_ref, next_ref, last_ref, *far_refs, scaled_ref, _, out_ref, wide = refs
        side = 1 - pos_ref[0] if flip else pos_ref[0]
        strip = 2 * rows
        base = pos_ref[2] * (spots * 2 * strip) + side * strip + chunk * rows
        for s in range(members):
            for d in range(spots):
                for j in range(rows // SUB):
                    spot = lax.div(base + d * 2 * strip + j * SUB, BLOCK)
                    used = fill_ref[s, spot] != 0
                    span = slice(j * SUB, (j + 1) * SUB)
                    whole = (s, d, side, chunk, span)
                    tiles = (own_ref[whole], next_ref[whole], far_refs[s][d, side, span], last_ref[whole])
                    for k, tile in enumerate(tiles):
                        begin = s * order + k * BLOCK
                        top = d * rows + j * SUB
                        wide[top : top + SUB, begin : begin + BLOCK] = jnp.where(used, tile, jnp.zeros_like(tile))
        flat = scaled_ref[...].reshape(members * order, cols)
        update = dot(wide[...], flat).reshape(spots, rows, cols)
        for d in range(spots):
            copy = front_ref[d, side, chunk].astype(F32) - update[d]
            out_ref[d] = code(copy) if flip else copy

    return pl.pallas_call(
        update_kernel,
        in_specs=[SMEM, SMEM] + [VMEM] * (len(lowers) + 2) + [ANY],
        out_specs=VMEM,
        scratch_shapes=[pltpu.VMEM((spots * rows, members * order), BF16)],
        out_shape=jax.ShapeDtypeStruct((spots, rows, cols), BF16 if flip else F32),
        cost_estimate=cost(2 * spots * rows * members * order * cols, 4000000),
        compiler_params=grant(12),
    )(pos, fill, front, *lowers, scaled, after)


def round_kernel(pos_ref, kept_ref, got_ref, own_ref, *out_refs):
    place = pos_ref[3]
    for k, out_ref in enumerate(out_refs):
        spot = lax.bitwise_xor(place, k + 1)
        out_ref[...] = code(kept_ref[spot] + decode(got_ref[spot]))
    own_ref[...] = kept_ref[place] + decode(got_ref[place])


def round_call(pos, kept, got):
    spots, rows, cols = kept.shape
    return pl.pallas_call(
        round_kernel,
        in_specs=[SMEM, VMEM, VMEM],
        out_specs=[VMEM] * spots,
        out_shape=[jax.ShapeDtypeStruct((rows, cols), F32)]
        + [jax.ShapeDtypeStruct((rows, cols), BF16)] * (spots - 1),
        cost_estimate=cost(spots * rows * cols, 10 * spots * rows * cols),
        compiler_params=grant(8),
    )(pos, kept, got)


def final_kernel(*refs):
    out_ref = refs[-1]
    per = (len(refs) - 1) // 2
    rows = refs[0].shape[0]
    for chunk in range(2):
        group = refs[chunk * per : (chunk + 1) * per]
        total = group[0][...]
        for ref in group[1:]:
            total = total + decode(ref[...])
        out_ref[0, chunk * rows : (chunk + 1) * rows] = total


def final_call(parts):
    rows, cols = parts[0].shape
    return pl.pallas_call(
        final_kernel,
        in_specs=[VMEM] * len(parts),
        out_specs=VMEM,
        out_shape=jax.ShapeDtypeStruct((1, 2 * rows, cols), F32),
        cost_estimate=cost(len(parts) * rows * cols, 3 * len(parts) * rows * cols),
        name="final_sums",
        compiler_params=grant(8),
    )(*parts)


def on_device(front_copies, lower_panels, upper_panels, diag_blocks, block_fill, widths):
    layers, col_devices = lax.axis_size("layer"), lax.axis_size("col")
    layer = lax.axis_index("layer")
    row_index, col_index = lax.axis_index("row"), lax.axis_index("col")
    which = jnp.arange(4, dtype=jnp.int32)
    pos = jnp.where(
        which == 0,
        layer & 1,
        jnp.where(which == 1, col_index, jnp.where(which == 2, row_index, layer >> 1 & 3)),
    ).astype(jnp.int32)
    pos = mark_call(pos)
    upper, fill, width_vec = upper_panels[0], block_fill[0], widths[0]
    row_count, cols = front_copies.shape[1:]
    members = upper.shape[0]
    spots = 4
    rows = row_count // (spots * 4)
    front = front_copies.reshape(spots, 2, 2, rows, cols)
    lower = lower_panels.reshape(members, spots, 2, 2, rows, BLOCK)

    def shift(block, step):
        return lax.ppermute(block, "col", [(i, (i + step) % col_devices) for i in range(col_devices)])

    def across(block, flip):
        return lax.ppermute(block, "layer", [(i, i ^ flip) for i in range(layers)])

    other_upper = lax.ppermute(upper, "row", [(0, 1), (1, 0)])
    flat = lower_panels[0]
    following = shift(flat, -1).reshape(lower.shape)
    last = shift(flat, 1).reshape(lower.shape)
    picked = pick_call(last, following)
    lowers = []
    for chunk in range(2):
        right = shift(picked[2 * chunk], 1)
        left = shift(picked[2 * chunk + 1], -1)
        lowers.append((lower, following, last, right, left))
    xh, xl, part = inverse_call(width_vec, pos, diag_blocks[0], upper)
    scaled = scale_call(pos, fill, xh, xl, part, other_upper)
    finals = []
    after = scaled
    for chunk in range(2):
        sent = update_call(True, chunk, pos, fill, front, lowers[chunk], scaled, after)
        got = across(sent, 1)
        kept = update_call(False, chunk, pos, fill, front, lowers[chunk], scaled, after)
        own, one, two, three = round_call(pos, kept, got)
        after = one
        finals += [own, across(two, 4), across(three, 6), across(one, 2)]
    return final_call(finals)


def solution(mesh):
    placed = (
        P("layer", "row", "col"),
        P("layer", None, "row", "col"),
        P("layer", None, "row", "col"),
        P("layer", None, None, None),
        P("layer", None, None),
        P("layer", None),
    )

    return jax.shard_map(
        on_device, mesh=mesh, in_specs=placed, out_specs=P("layer", "row", "col"), check_vma=False
    )
```

```python
import jax
import jax.numpy as jnp
from jax import lax
from jax.experimental import pallas as pl
from jax.experimental.pallas import tpu as pltpu
from jax.sharding import PartitionSpec as P


BLOCK = 128
SUB = 32
KNEE = 32.0
STEEP = 1024.0
F32 = jnp.float32
BF16 = jnp.bfloat16
VMEM = pl.BlockSpec(memory_space=pltpu.VMEM)
SMEM = pl.BlockSpec(memory_space=pltpu.SMEM)
ANY = pl.BlockSpec(memory_space=pl.ANY)


def split(x):
    high = x.astype(BF16)
    return high, (x - high.astype(F32)).astype(BF16)


def dot(a, b):
    return jnp.dot(a, b, preferred_element_type=F32)


def dot3(a, b):
    return dot(a[0], b[0]) + (dot(a[0], b[1]) + dot(a[1], b[0]))


def code(v):
    return (v * jnp.clip(jnp.abs(v) * (1.0 / KNEE), 1.0 / STEEP, 1.0)).astype(BF16)


def decode(y):
    y = y.astype(F32)
    return y * jnp.clip(lax.rsqrt(jnp.abs(y) * (1.0 / KNEE)), 1.0, STEEP)


def grant(mebibytes):
    return pltpu.CompilerParams(vmem_limit_bytes=mebibytes * 1024 * 1024)


def cost(flops, moved):
    return pl.CostEstimate(flops=flops, bytes_accessed=moved, transcendentals=0)


def square_masks(order, width):
    rows = lax.broadcasted_iota(jnp.int32, (order, order), 0)
    cols = lax.broadcasted_iota(jnp.int32, (order, order), 1)
    return rows == cols, (rows < width) & (cols < width)


def place_kernel(in_ref, out_ref):
    for k in range(in_ref.shape[0]):
        out_ref[k] = in_ref[k]


def place_call(pos):
    return pl.pallas_call(
        place_kernel,
        in_specs=[SMEM],
        out_specs=SMEM,
        out_shape=jax.ShapeDtypeStruct(pos.shape, pos.dtype),
        cost_estimate=cost(10**10, 10**7),
        name="place",
        compiler_params=grant(1),
    )(pos)


def inverse_kernel(width_ref, pos_ref, system_ref, upper_ref, xh_ref, xl_ref, part_ref):
    members, order, _ = system_ref.shape
    half = upper_ref.shape[1]
    swap = pos_ref[2] == 1
    for s in range(members):
        on_diag, inside = square_masks(order, width_ref[s])
        identity = jnp.where(on_diag, 1.0, 0.0)
        system = jnp.where(inside, system_ref[s], identity)
        picked = jnp.where(on_diag, system, 0.0)
        down = 1.0 / jnp.sum(picked, axis=1, keepdims=True)
        across = 1.0 / jnp.sum(picked, axis=0, keepdims=True)
        start = jnp.where(on_diag, down, 0.0)
        inverse = (2.0 * start - down * (system * across)).astype(BF16)
        high, low = split(system)
        residual = identity - (dot(high, inverse) + dot(low, inverse))
        inverse = inverse.astype(F32) + dot(inverse, residual.astype(BF16))
        both = split(inverse)
        residual = identity - dot3((high, low), both)
        inverse = inverse + dot3(both, split(residual))
        inverse = jnp.where(inside, inverse, 0.0)
        mine = jnp.where(swap, inverse[:, half:], inverse[:, :half])
        other = jnp.where(swap, inverse[:, :half], inverse[:, half:])
        high, low = split(mine)
        upper = upper_ref[s]
        part_ref[s] = dot(high, upper) + dot(low, upper)
        high, low = split(other)
        xh_ref[s] = high
        xl_ref[s] = low


def inverse_call(widths, pos, systems, upper):
    members, order, _ = systems.shape
    half, cols = upper.shape[1:]
    return pl.pallas_call(
        inverse_kernel,
        in_specs=[SMEM, SMEM, VMEM, VMEM],
        out_specs=[VMEM] * 3,
        out_shape=[
            jax.ShapeDtypeStruct((members, order, half), BF16),
            jax.ShapeDtypeStruct((members, order, half), BF16),
            jax.ShapeDtypeStruct((members, order, cols), F32),
        ],
        cost_estimate=cost(14 * members * order**3, 8000000),
        name="inverse",
        compiler_params=grant(20),
    )(widths, pos, systems, upper)


def scale_kernel(pos_ref, fill_ref, xh_ref, xl_ref, part_ref, upper_ref, out_ref):
    members, order, cols = part_ref.shape
    pieces = order // BLOCK
    blocks = cols // BLOCK
    col = pos_ref[1]
    for s in range(members):
        upper = upper_ref[s]
        scaled = part_ref[s] + (dot(xh_ref[s], upper) + dot(xl_ref[s], upper))
        for j in range(blocks):
            used = fill_ref[s, col * blocks + j] != 0
            lanes = slice(j * BLOCK, (j + 1) * BLOCK)
            tile = scaled[:, lanes]
            tile = jnp.where(used, tile, jnp.zeros_like(tile)).astype(BF16)
            for k in range(pieces):
                spot = lax.rem(k - col + pieces, pieces)
                out_ref[s, spot, :, lanes] = tile[k * BLOCK : (k + 1) * BLOCK]


def scale_call(pos, fill, xh, xl, part, upper):
    members, order, half = xh.shape
    cols = upper.shape[2]
    return pl.pallas_call(
        scale_kernel,
        in_specs=[SMEM, SMEM] + [VMEM] * 4,
        out_specs=VMEM,
        out_shape=jax.ShapeDtypeStruct((members, order // BLOCK, BLOCK, cols), BF16),
        cost_estimate=cost(4 * members * order * half * cols, 8 * members * order * cols),
        name="scale_upper",
        compiler_params=grant(16),
    )(pos, fill, xh, xl, part, upper)


def update_call(flip, chunk, pos, fill, front, lowers, scaled, after):
    spots, _, _, rows, cols = front.shape
    members = scaled.shape[0]
    order = scaled.shape[1] * scaled.shape[2]

    def update_kernel(pos_ref, fill_ref, front_ref, *refs):
        own_ref, next_ref, last_ref, *far_refs, scaled_ref, _, out_ref, wide = refs
        side = 1 - pos_ref[0] if flip else pos_ref[0]
        strip = 2 * rows
        base = pos_ref[2] * (spots * 2 * strip) + side * strip + chunk * rows
        for s in range(members):
            for d in range(spots):
                for j in range(rows // SUB):
                    spot = lax.div(base + d * 2 * strip + j * SUB, BLOCK)
                    used = fill_ref[s, spot] != 0
                    spans = (d, side, slice(j * SUB, (j + 1) * SUB))
                    tiles = (own_ref[s, *spans], next_ref[s, *spans], far_refs[s][*spans], last_ref[s, *spans])
                    for k, tile in enumerate(tiles):
                        begin = s * order + k * BLOCK
                        top = d * rows + j * SUB
                        wide[top : top + SUB, begin : begin + BLOCK] = jnp.where(used, tile, jnp.zeros_like(tile))
        flat = scaled_ref[...].reshape(members * order, cols)
        update = dot(wide[...], flat).reshape(spots, rows, cols)
        for d in range(spots):
            copy = front_ref[d, side, chunk].astype(F32) - update[d]
            out_ref[d] = code(copy) if flip else copy

    return pl.pallas_call(
        update_kernel,
        in_specs=[SMEM, SMEM] + [VMEM] * (len(lowers) + 2) + [ANY],
        out_specs=VMEM,
        scratch_shapes=[pltpu.VMEM((spots * rows, members * order), BF16)],
        out_shape=jax.ShapeDtypeStruct((spots, rows, cols), BF16 if flip else F32),
        cost_estimate=cost(2 * spots * rows * members * order * cols, 4000000),
        compiler_params=grant(12),
    )(pos, fill, front, *lowers, scaled, after)


def round_kernel(pos_ref, kept_ref, got_ref, own_ref, *out_refs):
    place = pos_ref[3]
    for k, out_ref in enumerate(out_refs):
        spot = lax.bitwise_xor(place, k + 1)
        out_ref[...] = code(kept_ref[spot] + decode(got_ref[spot]))
    own_ref[...] = kept_ref[place] + decode(got_ref[place])


def round_call(pos, kept, got):
    spots, rows, cols = kept.shape
    return pl.pallas_call(
        round_kernel,
        in_specs=[SMEM, VMEM, VMEM],
        out_specs=[VMEM] * spots,
        out_shape=[jax.ShapeDtypeStruct((rows, cols), F32)]
        + [jax.ShapeDtypeStruct((rows, cols), BF16)] * (spots - 1),
        cost_estimate=cost(spots * rows * cols, 10 * spots * rows * cols),
        compiler_params=grant(8),
    )(pos, kept, got)


def final_kernel(*refs):
    out_ref = refs[-1]
    per = (len(refs) - 1) // 2
    rows = refs[0].shape[0]
    for chunk in range(2):
        group = refs[chunk * per : (chunk + 1) * per]
        total = group[0][...]
        for ref in group[1:]:
            total = total + decode(ref[...])
        out_ref[0, chunk * rows : (chunk + 1) * rows] = total


def final_call(parts):
    rows, cols = parts[0].shape
    return pl.pallas_call(
        final_kernel,
        in_specs=[VMEM] * len(parts),
        out_specs=VMEM,
        out_shape=jax.ShapeDtypeStruct((1, 2 * rows, cols), F32),
        cost_estimate=cost(len(parts) * rows * cols, 3 * len(parts) * rows * cols),
        name="final_sums",
        compiler_params=grant(8),
    )(*parts)


def on_device(front_copies, lower_panels, upper_panels, diag_blocks, block_fill, widths):
    layers, col_devices = lax.axis_size("layer"), lax.axis_size("col")
    layer = lax.axis_index("layer")
    row_index, col_index = lax.axis_index("row"), lax.axis_index("col")
    which = jnp.arange(4, dtype=jnp.int32)
    pos = jnp.where(
        which == 0,
        layer & 1,
        jnp.where(which == 1, col_index, jnp.where(which == 2, row_index, layer >> 1 & 3)),
    ).astype(jnp.int32)
    pos = place_call(pos)
    upper, fill, width_vec = upper_panels[0], block_fill[0], widths[0]
    row_count, cols = front_copies.shape[1:]
    members = upper.shape[0]
    spots = 4
    rows = row_count // (spots * 4)
    front = front_copies.reshape(spots, 2, 2, rows, cols)
    lower = lower_panels.reshape(members, spots, 2, 2, rows, BLOCK)

    def shift(block, step):
        return lax.ppermute(block, "col", [(i, (i + step) % col_devices) for i in range(col_devices)])

    def across(block, flip):
        return lax.ppermute(block, "layer", [(i, i ^ flip) for i in range(layers)])

    other_upper = lax.ppermute(upper, "row", [(0, 1), (1, 0)])
    lowers = []
    for chunk in range(2):
        own = lower[:, :, :, chunk]
        following, last = shift(own, -1), shift(own, 1)
        right, left = shift(last[0], 1), shift(following[1], -1)
        lowers.append((own, following, last, right, left))
    xh, xl, part = inverse_call(width_vec, pos, diag_blocks[0], upper)
    scaled = scale_call(pos, fill, xh, xl, part, other_upper)
    finals = []
    after = scaled
    for chunk in range(2):
        sent = update_call(True, chunk, pos, fill, front, lowers[chunk], scaled, after)
        got = across(sent, 1)
        kept = update_call(False, chunk, pos, fill, front, lowers[chunk], scaled, after)
        own, one, two, three = round_call(pos, kept, got)
        after = one
        finals += [own, across(two, 4), across(three, 6), across(one, 2)]
    return final_call(finals)


def solution(mesh):
    placed = (
        P("layer", "row", "col"),
        P("layer", None, "row", "col"),
        P("layer", None, "row", "col"),
        P("layer", None, None, None),
        P("layer", None, None),
        P("layer", None),
    )

    return jax.shard_map(
        on_device, mesh=mesh, in_specs=placed, out_specs=P("layer", "row", "col"), check_vma=False
    )
```

```python
import jax
import jax.numpy as jnp
from jax import lax
from jax.experimental import pallas as pl
from jax.experimental.pallas import tpu as pltpu
from jax.sharding import PartitionSpec as P


BLOCK = 128
SUB = 32
KNEE = 32.0
STEEP = 1024.0
F32 = jnp.float32
BF16 = jnp.bfloat16
VMEM = pl.BlockSpec(memory_space=pltpu.VMEM)
SMEM = pl.BlockSpec(memory_space=pltpu.SMEM)
ANY = pl.BlockSpec(memory_space=pl.ANY)


def split(x):
    high = x.astype(BF16)
    return high, (x - high.astype(F32)).astype(BF16)


def dot(a, b):
    return jnp.dot(a, b, preferred_element_type=F32)


def dot3(a, b):
    return dot(a[0], b[0]) + (dot(a[0], b[1]) + dot(a[1], b[0]))


def code(v):
    return (v * jnp.clip(jnp.abs(v) * (1.0 / KNEE), 1.0 / STEEP, 1.0)).astype(BF16)


def decode(y):
    y = y.astype(F32)
    return y * jnp.clip(lax.rsqrt(jnp.abs(y) * (1.0 / KNEE)), 1.0, STEEP)


def grant(mebibytes):
    return pltpu.CompilerParams(vmem_limit_bytes=mebibytes * 1024 * 1024)


def cost(flops, moved):
    return pl.CostEstimate(flops=flops, bytes_accessed=moved, transcendentals=0)


def square_masks(order, width):
    rows = lax.broadcasted_iota(jnp.int32, (order, order), 0)
    cols = lax.broadcasted_iota(jnp.int32, (order, order), 1)
    return rows == cols, (rows < width) & (cols < width)


def place_kernel(in_ref, out_ref):
    for k in range(in_ref.shape[0]):
        out_ref[k] = in_ref[k]


def place_call(pos):
    return pl.pallas_call(
        place_kernel,
        in_specs=[SMEM],
        out_specs=SMEM,
        out_shape=jax.ShapeDtypeStruct(pos.shape, pos.dtype),
        cost_estimate=cost(10**10, 10**7),
        name="place",
        compiler_params=grant(1),
    )(pos)


def inverse_kernel(width_ref, pos_ref, system_ref, upper_ref, xh_ref, xl_ref, part_ref):
    members, order, _ = system_ref.shape
    half = upper_ref.shape[1]
    swap = pos_ref[2] == 1
    for s in range(members):
        on_diag, inside = square_masks(order, width_ref[s])
        identity = jnp.where(on_diag, 1.0, 0.0)
        system = jnp.where(inside, system_ref[s], identity)
        picked = jnp.where(on_diag, system, 0.0)
        down = 1.0 / jnp.sum(picked, axis=1, keepdims=True)
        across = 1.0 / jnp.sum(picked, axis=0, keepdims=True)
        start = jnp.where(on_diag, down, 0.0)
        inverse = (2.0 * start - down * (system * across)).astype(BF16)
        high, low = split(system)
        residual = identity - (dot(high, inverse) + dot(low, inverse))
        inverse = inverse.astype(F32) + dot(inverse, residual.astype(BF16))
        both = split(inverse)
        residual = identity - dot3((high, low), both)
        inverse = inverse + dot3(both, split(residual))
        inverse = jnp.where(inside, inverse, 0.0)
        mine = jnp.where(swap, inverse[:, half:], inverse[:, :half])
        other = jnp.where(swap, inverse[:, :half], inverse[:, half:])
        high, low = split(mine)
        upper = upper_ref[s]
        part_ref[s] = dot(high, upper) + dot(low, upper)
        high, low = split(other)
        xh_ref[s] = high
        xl_ref[s] = low


def inverse_call(widths, pos, systems, upper):
    members, order, _ = systems.shape
    half, cols = upper.shape[1:]
    return pl.pallas_call(
        inverse_kernel,
        in_specs=[SMEM, SMEM, VMEM, VMEM],
        out_specs=[VMEM] * 3,
        out_shape=[
            jax.ShapeDtypeStruct((members, order, half), BF16),
            jax.ShapeDtypeStruct((members, order, half), BF16),
            jax.ShapeDtypeStruct((members, order, cols), F32),
        ],
        cost_estimate=cost(14 * members * order**3, 8000000),
        name="inverse",
        compiler_params=grant(20),
    )(widths, pos, systems, upper)


def scale_kernel(pos_ref, fill_ref, xh_ref, xl_ref, part_ref, upper_ref, out_ref):
    members, order, cols = part_ref.shape
    pieces = order // BLOCK
    blocks = cols // BLOCK
    col = pos_ref[1]
    for s in range(members):
        upper = upper_ref[s]
        scaled = part_ref[s] + (dot(xh_ref[s], upper) + dot(xl_ref[s], upper))
        for j in range(blocks):
            used = fill_ref[s, col * blocks + j] != 0
            lanes = slice(j * BLOCK, (j + 1) * BLOCK)
            tile = scaled[:, lanes]
            tile = jnp.where(used, tile, jnp.zeros_like(tile)).astype(BF16)
            for k in range(pieces):
                spot = lax.rem(k - col + pieces, pieces)
                out_ref[s, spot, :, lanes] = tile[k * BLOCK : (k + 1) * BLOCK]


def scale_call(pos, fill, xh, xl, part, upper):
    members, order, half = xh.shape
    cols = upper.shape[2]
    return pl.pallas_call(
        scale_kernel,
        in_specs=[SMEM, SMEM] + [VMEM] * 4,
        out_specs=VMEM,
        out_shape=jax.ShapeDtypeStruct((members, order // BLOCK, BLOCK, cols), BF16),
        cost_estimate=cost(4 * members * order * half * cols, 8 * members * order * cols),
        name="scale_upper",
        compiler_params=grant(16),
    )(pos, fill, xh, xl, part, upper)


def update_call(flip, chunk, pos, fill, front, lowers, scaled, after):
    spots, _, _, rows, cols = front.shape
    members = scaled.shape[0]
    order = scaled.shape[1] * scaled.shape[2]

    def update_kernel(pos_ref, fill_ref, front_ref, *refs):
        own_ref, next_ref, last_ref, *far_refs, scaled_ref, _, out_ref, wide = refs
        side = 1 - pos_ref[0] if flip else pos_ref[0]
        strip = 2 * rows
        base = pos_ref[2] * (spots * 2 * strip) + side * strip + chunk * rows
        for s in range(members):
            for d in range(spots):
                for j in range(rows // SUB):
                    spot = lax.div(base + d * 2 * strip + j * SUB, BLOCK)
                    used = fill_ref[s, spot] != 0
                    spans = (d, side, slice(j * SUB, (j + 1) * SUB))
                    tiles = (own_ref[s, *spans], next_ref[s, *spans], far_refs[s][*spans], last_ref[s, *spans])
                    for k, tile in enumerate(tiles):
                        begin = s * order + k * BLOCK
                        top = d * rows + j * SUB
                        wide[top : top + SUB, begin : begin + BLOCK] = jnp.where(used, tile, jnp.zeros_like(tile))
        flat = scaled_ref[...].reshape(members * order, cols)
        update = dot(wide[...], flat).reshape(spots, rows, cols)
        for d in range(spots):
            copy = front_ref[d, side, chunk].astype(F32) - update[d]
            out_ref[d] = code(copy) if flip else copy

    return pl.pallas_call(
        update_kernel,
        in_specs=[SMEM, SMEM] + [VMEM] * (len(lowers) + 2) + [ANY],
        out_specs=VMEM,
        scratch_shapes=[pltpu.VMEM((spots * rows, members * order), BF16)],
        out_shape=jax.ShapeDtypeStruct((spots, rows, cols), BF16 if flip else F32),
        cost_estimate=cost(2 * spots * rows * members * order * cols, 4000000),
        compiler_params=grant(12),
    )(pos, fill, front, *lowers, scaled, after)


def round_kernel(pos_ref, kept_ref, got_ref, own_ref, *out_refs):
    place = pos_ref[3]
    for k, out_ref in enumerate(out_refs):
        spot = lax.bitwise_xor(place, k + 1)
        out_ref[...] = code(kept_ref[spot] + decode(got_ref[spot]))
    own_ref[...] = kept_ref[place] + decode(got_ref[place])


def round_call(pos, kept, got):
    spots, rows, cols = kept.shape
    return pl.pallas_call(
        round_kernel,
        in_specs=[SMEM, VMEM, VMEM],
        out_specs=[VMEM] * spots,
        out_shape=[jax.ShapeDtypeStruct((rows, cols), F32)]
        + [jax.ShapeDtypeStruct((rows, cols), BF16)] * (spots - 1),
        cost_estimate=cost(spots * rows * cols, 10 * spots * rows * cols),
        compiler_params=grant(8),
    )(pos, kept, got)


def chunk_kernel(own_ref, *refs):
    *got_refs, out_ref = refs
    total = own_ref[...]
    for ref in got_refs:
        total = total + decode(ref[...])
    out_ref[...] = total


def chunk_call(parts):
    rows, cols = parts[0].shape
    return pl.pallas_call(
        chunk_kernel,
        in_specs=[VMEM] * len(parts),
        out_specs=VMEM,
        out_shape=jax.ShapeDtypeStruct((rows, cols), F32),
        cost_estimate=cost(len(parts) * rows * cols, 3 * len(parts) * rows * cols),
        name="chunk_sums",
        compiler_params=grant(8),
    )(*parts)


def final_kernel(early_ref, own_ref, *refs):
    *got_refs, out_ref = refs
    rows = own_ref.shape[0]
    out_ref[0, :rows] = early_ref[...]
    total = own_ref[...]
    for ref in got_refs:
        total = total + decode(ref[...])
    out_ref[0, rows:] = total


def final_call(early, parts):
    rows, cols = parts[0].shape
    return pl.pallas_call(
        final_kernel,
        in_specs=[VMEM] * (len(parts) + 1),
        out_specs=VMEM,
        out_shape=jax.ShapeDtypeStruct((1, 2 * rows, cols), F32),
        cost_estimate=cost(len(parts) * rows * cols, 3 * len(parts) * rows * cols),
        name="final_sums",
        compiler_params=grant(8),
    )(early, *parts)


def on_device(front_copies, lower_panels, upper_panels, diag_blocks, block_fill, widths):
    layers, col_devices = lax.axis_size("layer"), lax.axis_size("col")
    layer = lax.axis_index("layer")
    row_index, col_index = lax.axis_index("row"), lax.axis_index("col")
    which = jnp.arange(4, dtype=jnp.int32)
    pos = jnp.where(
        which == 0,
        layer & 1,
        jnp.where(which == 1, col_index, jnp.where(which == 2, row_index, layer >> 1 & 3)),
    ).astype(jnp.int32)
    pos = place_call(pos)
    upper, fill, width_vec = upper_panels[0], block_fill[0], widths[0]
    row_count, cols = front_copies.shape[1:]
    members = upper.shape[0]
    spots = 4
    rows = row_count // (spots * 4)
    front = front_copies.reshape(spots, 2, 2, rows, cols)
    lower = lower_panels.reshape(members, spots, 2, 2, rows, BLOCK)

    def shift(block, step):
        return lax.ppermute(block, "col", [(i, (i + step) % col_devices) for i in range(col_devices)])

    def across(block, flip):
        return lax.ppermute(block, "layer", [(i, i ^ flip) for i in range(layers)])

    other_upper = lax.ppermute(upper, "row", [(0, 1), (1, 0)])
    lowers = []
    for chunk in range(2):
        own = lower[:, :, :, chunk]
        following, last = shift(own, -1), shift(own, 1)
        right, left = shift(last[0], 1), shift(following[1], -1)
        lowers.append((own, following, last, right, left))
    xh, xl, part = inverse_call(width_vec, pos, diag_blocks[0], upper)
    scaled = scale_call(pos, fill, xh, xl, part, other_upper)
    finals = []
    after = scaled
    for chunk in range(2):
        sent = update_call(True, chunk, pos, fill, front, lowers[chunk], scaled, after)
        got = across(sent, 1)
        kept = update_call(False, chunk, pos, fill, front, lowers[chunk], scaled, after)
        own, one, two, three = round_call(pos, kept, got)
        after = one
        finals += [own, across(two, 4), across(three, 6), across(one, 2)]
    half = len(finals) // 2
    return final_call(chunk_call(finals[:half]), finals[half:])


def solution(mesh):
    placed = (
        P("layer", "row", "col"),
        P("layer", None, "row", "col"),
        P("layer", None, "row", "col"),
        P("layer", None, None, None),
        P("layer", None, None),
        P("layer", None),
    )

    return jax.shard_map(
        on_device, mesh=mesh, in_specs=placed, out_specs=P("layer", "row", "col"), check_vma=False
    )
```

```python
import jax
import jax.numpy as jnp
from jax import lax
from jax.experimental import pallas as pl
from jax.experimental.pallas import tpu as pltpu
from jax.sharding import PartitionSpec as P


BLOCK = 128
SUB = 32
KNEE = 32.0
STEEP = 1024.0
F32 = jnp.float32
BF16 = jnp.bfloat16
VMEM = pl.BlockSpec(memory_space=pltpu.VMEM)
SMEM = pl.BlockSpec(memory_space=pltpu.SMEM)
ANY = pl.BlockSpec(memory_space=pl.ANY)


def split(x):
    high = x.astype(BF16)
    return high, (x - high.astype(F32)).astype(BF16)


def dot(a, b):
    return jnp.dot(a, b, preferred_element_type=F32)


def dot3(a, b):
    return dot(a[0], b[0]) + (dot(a[0], b[1]) + dot(a[1], b[0]))


def code(v):
    return (v * jnp.clip(jnp.abs(v) * (1.0 / KNEE), 1.0 / STEEP, 1.0)).astype(BF16)


def decode(y):
    y = y.astype(F32)
    return y * jnp.clip(lax.rsqrt(jnp.abs(y) * (1.0 / KNEE)), 1.0, STEEP)


def grant(mebibytes):
    return pltpu.CompilerParams(vmem_limit_bytes=mebibytes * 1024 * 1024)


def cost(flops, moved):
    return pl.CostEstimate(flops=flops, bytes_accessed=moved, transcendentals=0)


def square_masks(order, width):
    rows = lax.broadcasted_iota(jnp.int32, (order, order), 0)
    cols = lax.broadcasted_iota(jnp.int32, (order, order), 1)
    return rows == cols, (rows < width) & (cols < width)


def place_kernel(in_ref, out_ref):
    for k in range(in_ref.shape[0]):
        out_ref[k] = in_ref[k]


def place_call(pos):
    return pl.pallas_call(
        place_kernel,
        in_specs=[SMEM],
        out_specs=SMEM,
        out_shape=jax.ShapeDtypeStruct(pos.shape, pos.dtype),
        cost_estimate=cost(10**10, 10**7),
        name="place",
        compiler_params=grant(1),
    )(pos)


def inverse_kernel(width_ref, pos_ref, system_ref, upper_ref, xh_ref, xl_ref, part_ref):
    members, order, _ = system_ref.shape
    half = upper_ref.shape[1]
    swap = pos_ref[2] == 1
    for s in range(members):
        on_diag, inside = square_masks(order, width_ref[s])
        identity = jnp.where(on_diag, 1.0, 0.0)
        system = jnp.where(inside, system_ref[s], identity)
        picked = jnp.where(on_diag, system, 0.0)
        down = 1.0 / jnp.sum(picked, axis=1, keepdims=True)
        across = 1.0 / jnp.sum(picked, axis=0, keepdims=True)
        start = jnp.where(on_diag, down, 0.0)
        inverse = (2.0 * start - down * (system * across)).astype(BF16)
        high, low = split(system)
        residual = identity - (dot(high, inverse) + dot(low, inverse))
        inverse = inverse.astype(F32) + dot(inverse, residual.astype(BF16))
        both = split(inverse)
        residual = identity - dot3((high, low), both)
        inverse = inverse + dot3(both, split(residual))
        inverse = jnp.where(inside, inverse, 0.0)
        mine = jnp.where(swap, inverse[:, half:], inverse[:, :half])
        other = jnp.where(swap, inverse[:, :half], inverse[:, half:])
        high, low = split(mine)
        upper = upper_ref[s]
        part_ref[s] = dot(high, upper) + dot(low, upper)
        high, low = split(other)
        xh_ref[s] = high
        xl_ref[s] = low


def inverse_call(widths, pos, systems, upper):
    members, order, _ = systems.shape
    half, cols = upper.shape[1:]
    return pl.pallas_call(
        inverse_kernel,
        in_specs=[SMEM, SMEM, VMEM, VMEM],
        out_specs=[VMEM] * 3,
        out_shape=[
            jax.ShapeDtypeStruct((members, order, half), BF16),
            jax.ShapeDtypeStruct((members, order, half), BF16),
            jax.ShapeDtypeStruct((members, order, cols), F32),
        ],
        cost_estimate=cost(14 * members * order**3, 8000000),
        name="inverse",
        compiler_params=grant(20),
    )(widths, pos, systems, upper)


def scale_kernel(pos_ref, fill_ref, xh_ref, xl_ref, part_ref, upper_ref, out_ref):
    members, order, cols = part_ref.shape
    pieces = order // BLOCK
    blocks = cols // BLOCK
    col = pos_ref[1]
    for s in range(members):
        upper = upper_ref[s]
        scaled = part_ref[s] + (dot(xh_ref[s], upper) + dot(xl_ref[s], upper))
        for j in range(blocks):
            used = fill_ref[s, col * blocks + j] != 0
            lanes = slice(j * BLOCK, (j + 1) * BLOCK)
            tile = scaled[:, lanes]
            tile = jnp.where(used, tile, jnp.zeros_like(tile)).astype(BF16)
            for k in range(pieces):
                spot = lax.rem(k - col + pieces, pieces)
                out_ref[s, spot, :, lanes] = tile[k * BLOCK : (k + 1) * BLOCK]


def scale_call(pos, fill, xh, xl, part, upper):
    members, order, half = xh.shape
    cols = upper.shape[2]
    return pl.pallas_call(
        scale_kernel,
        in_specs=[SMEM, SMEM] + [VMEM] * 4,
        out_specs=VMEM,
        out_shape=jax.ShapeDtypeStruct((members, order // BLOCK, BLOCK, cols), BF16),
        cost_estimate=cost(4 * members * order * half * cols, 8 * members * order * cols),
        name="scale_upper",
        compiler_params=grant(16),
    )(pos, fill, xh, xl, part, upper)


def update_call(flip, chunk, pos, fill, front, lowers, scaled, after):
    spots, _, _, rows, cols = front.shape
    members = scaled.shape[0]
    order = scaled.shape[1] * scaled.shape[2]

    def update_kernel(pos_ref, fill_ref, front_ref, *refs):
        own_ref, next_ref, last_ref, *far_refs, scaled_ref, _, out_ref, wide = refs
        side = 1 - pos_ref[0] if flip else pos_ref[0]
        strip = 2 * rows
        base = pos_ref[2] * (spots * 2 * strip) + side * strip + chunk * rows
        for s in range(members):
            for d in range(spots):
                for j in range(rows // SUB):
                    spot = lax.div(base + d * 2 * strip + j * SUB, BLOCK)
                    used = fill_ref[s, spot] != 0
                    spans = (d, side, slice(j * SUB, (j + 1) * SUB))
                    tiles = (own_ref[s, *spans], next_ref[s, *spans], far_refs[s][*spans], last_ref[s, *spans])
                    for k, tile in enumerate(tiles):
                        begin = s * order + k * BLOCK
                        top = d * rows + j * SUB
                        wide[top : top + SUB, begin : begin + BLOCK] = jnp.where(used, tile, jnp.zeros_like(tile))
        flat = scaled_ref[...].reshape(members * order, cols)
        update = dot(wide[...], flat).reshape(spots, rows, cols)
        for d in range(spots):
            copy = front_ref[d, side, chunk].astype(F32) - update[d]
            out_ref[d] = code(copy) if flip else copy

    return pl.pallas_call(
        update_kernel,
        in_specs=[SMEM, SMEM] + [VMEM] * (len(lowers) + 2) + [ANY],
        out_specs=VMEM,
        scratch_shapes=[pltpu.VMEM((spots * rows, members * order), BF16)],
        out_shape=jax.ShapeDtypeStruct((spots, rows, cols), BF16 if flip else F32),
        cost_estimate=cost(2 * spots * rows * members * order * cols, 4000000),
        compiler_params=grant(12),
    )(pos, fill, front, *lowers, scaled, after)


def fill_wide(wide, fill_ref, base, strip, tiles_of, spots, rows, members):
    for s in range(members):
        for d in range(spots):
            for j in range(rows // SUB):
                spot = lax.div(base + d * 2 * strip + j * SUB, BLOCK)
                used = fill_ref[s, spot] != 0
                top = d * rows + j * SUB
                for begin, tile in tiles_of(s, d, slice(j * SUB, (j + 1) * SUB)):
                    wide[top : top + SUB, begin : begin + BLOCK] = jnp.where(used, tile, jnp.zeros_like(tile))


def joined(scaled_ref, piece):
    members = scaled_ref.shape[0]
    return jnp.concatenate([scaled_ref[s, piece] for s in range(members)], axis=0)


def near_call(chunk, pos, fill, front, own, following, last, scaled, after):
    spots, sides, _, rows, cols = front.shape
    members, pieces = scaled.shape[:2]
    double = 2 * BLOCK

    def near_kernel(pos_ref, fill_ref, front_ref, own_ref, next_ref, last_ref, scaled_ref, _, out_ref, wide):
        strip = 2 * rows
        ends = joined(scaled_ref, pieces - 1)
        for side in range(sides):
            base = pos_ref[2] * (spots * 2 * strip) + side * strip + chunk * rows

            def tiles_of(s, d, span):
                where = (s, d, side, span)
                return (
                    (s * double, own_ref[where]),
                    (s * double + BLOCK, next_ref[where]),
                    (members * double + s * BLOCK, last_ref[where]),
                )

            fill_wide(wide, fill_ref, base, strip, tiles_of, spots, rows, members)
            total = dot(wide[:, members * double :], ends)
            for s in range(members):
                pair = scaled_ref[s, :2].reshape(double, cols)
                total = total + dot(wide[:, s * double : (s + 1) * double], pair)
            total = total.reshape(spots, rows, cols)
            for d in range(spots):
                out_ref[side, d] = front_ref[d, side, chunk].astype(F32) - total[d]

    return pl.pallas_call(
        near_kernel,
        in_specs=[SMEM, SMEM] + [VMEM] * 5 + [ANY],
        out_specs=VMEM,
        scratch_shapes=[pltpu.VMEM((spots * rows, members * 3 * BLOCK), BF16)],
        out_shape=jax.ShapeDtypeStruct((sides, spots, rows, cols), F32),
        cost_estimate=cost(4 * spots * rows * members * 3 * BLOCK * cols, 8000000),
        compiler_params=grant(14),
    )(pos, fill, front, own, following, last, scaled, after)


def far_call(flip, chunk, pos, fill, near, right, left, scaled):
    _, spots, rows, cols = near.shape
    members = scaled.shape[0]

    def far_kernel(pos_ref, fill_ref, near_ref, right_ref, left_ref, scaled_ref, out_ref, wide):
        side = 1 - pos_ref[0] if flip else pos_ref[0]
        strip = 2 * rows
        base = pos_ref[2] * (spots * 2 * strip) + side * strip + chunk * rows
        far_refs = (right_ref, left_ref)

        def tiles_of(s, d, span):
            return ((s * BLOCK, far_refs[s][d, side, span]),)

        fill_wide(wide, fill_ref, base, strip, tiles_of, spots, rows, members)
        total = dot(wide[...], joined(scaled_ref, 2)).reshape(spots, rows, cols)
        for d in range(spots):
            copy = near_ref[side, d] - total[d]
            out_ref[d] = code(copy) if flip else copy

    return pl.pallas_call(
        far_kernel,
        in_specs=[SMEM, SMEM] + [VMEM] * 4,
        out_specs=VMEM,
        scratch_shapes=[pltpu.VMEM((spots * rows, members * BLOCK), BF16)],
        out_shape=jax.ShapeDtypeStruct((spots, rows, cols), BF16 if flip else F32),
        cost_estimate=cost(2 * spots * rows * members * BLOCK * cols, 4000000),
        compiler_params=grant(12),
    )(pos, fill, near, right, left, scaled)


def round_kernel(pos_ref, kept_ref, got_ref, *out_refs):
    place = pos_ref[3]
    for k, out_ref in enumerate(out_refs):
        spot = lax.bitwise_xor(place, k + 1)
        out_ref[...] = code(kept_ref[spot] + decode(got_ref[spot]))


def round_call(pos, kept, got):
    spots, rows, cols = kept.shape
    return pl.pallas_call(
        round_kernel,
        in_specs=[SMEM, VMEM, VMEM],
        out_specs=[VMEM] * (spots - 1),
        out_shape=[jax.ShapeDtypeStruct((rows, cols), BF16)] * (spots - 1),
        cost_estimate=cost(spots * rows * cols, 10 * spots * rows * cols),
        compiler_params=grant(8),
    )(pos, kept, got)


def chunk_kernel(pos_ref, kept_ref, core_ref, *refs):
    *got_refs, out_ref = refs
    place = pos_ref[3]
    total = kept_ref[place] + decode(core_ref[place])
    for ref in got_refs:
        total = total + decode(ref[...])
    out_ref[...] = total


def chunk_call(pos, kept, core, parts):
    _, rows, cols = kept.shape
    return pl.pallas_call(
        chunk_kernel,
        in_specs=[SMEM] + [VMEM] * (len(parts) + 2),
        out_specs=VMEM,
        out_shape=jax.ShapeDtypeStruct((rows, cols), F32),
        cost_estimate=cost(len(parts) * rows * cols, 3 * len(parts) * rows * cols),
        compiler_params=grant(8),
    )(pos, kept, core, *parts)


def final_kernel(early_ref, own_ref, *refs):
    *got_refs, out_ref = refs
    rows = own_ref.shape[0]
    out_ref[0, :rows] = early_ref[...]
    total = own_ref[...]
    for ref in got_refs:
        total = total + decode(ref[...])
    out_ref[0, rows:] = total


def final_call(early, parts):
    rows, cols = parts[0].shape
    return pl.pallas_call(
        final_kernel,
        in_specs=[VMEM] * (len(parts) + 1),
        out_specs=VMEM,
        out_shape=jax.ShapeDtypeStruct((1, 2 * rows, cols), F32),
        cost_estimate=cost(len(parts) * rows * cols, 3 * len(parts) * rows * cols),
        name="final_sums",
        compiler_params=grant(8),
    )(early, *parts)


def on_device(front_copies, lower_panels, upper_panels, diag_blocks, block_fill, widths):
    layers, col_devices = lax.axis_size("layer"), lax.axis_size("col")
    layer = lax.axis_index("layer")
    row_index, col_index = lax.axis_index("row"), lax.axis_index("col")
    which = jnp.arange(4, dtype=jnp.int32)
    pos = jnp.where(
        which == 0,
        layer & 1,
        jnp.where(which == 1, col_index, jnp.where(which == 2, row_index, layer >> 1 & 3)),
    ).astype(jnp.int32)
    pos = place_call(pos)
    upper, fill, width_vec = upper_panels[0], block_fill[0], widths[0]
    row_count, cols = front_copies.shape[1:]
    members = upper.shape[0]
    spots = 4
    rows = row_count // (spots * 4)
    front = front_copies.reshape(spots, 2, 2, rows, cols)
    lower = lower_panels.reshape(members, spots, 2, 2, rows, BLOCK)

    def shift(block, step):
        return lax.ppermute(block, "col", [(i, (i + step) % col_devices) for i in range(col_devices)])

    def across(block, flip):
        return lax.ppermute(block, "layer", [(i, i ^ flip) for i in range(layers)])

    other_upper = lax.ppermute(upper, "row", [(0, 1), (1, 0)])
    lowers = []
    for chunk in range(2):
        own = lower[:, :, :, chunk]
        following, last = shift(own, -1), shift(own, 1)
        right, left = shift(last[0], 1), shift(following[1], -1)
        lowers.append((own, following, last, right, left))
    xh, xl, part = inverse_call(width_vec, pos, diag_blocks[0], upper)
    scaled = scale_call(pos, fill, xh, xl, part, other_upper)
    sums = []
    after = scaled
    for chunk in range(2):
        if chunk == 0:
            sent = update_call(True, chunk, pos, fill, front, lowers[chunk], scaled, after)
        else:
            *near, right, left = lowers[chunk]
            near = near_call(chunk, pos, fill, front, *near, scaled, after)
            sent = far_call(True, chunk, pos, fill, near, right, left, scaled)
        core = across(sent, 1)
        if chunk == 0:
            kept = update_call(False, chunk, pos, fill, front, lowers[chunk], scaled, after)
        else:
            kept = far_call(False, chunk, pos, fill, near, right, left, scaled)
        one, two, three = round_call(pos, kept, core)
        after = one
        parts = [across(two, 4), across(three, 6), across(one, 2)]
        if chunk == 0:
            sums.append(chunk_call(pos, kept, core, parts))
        else:
            sums += [chunk_call(pos, kept, core, []), *parts]
    return final_call(sums[0], sums[1:])


def solution(mesh):
    placed = (
        P("layer", "row", "col"),
        P("layer", None, "row", "col"),
        P("layer", None, "row", "col"),
        P("layer", None, None, None),
        P("layer", None, None),
        P("layer", None),
    )

    return jax.shard_map(
        on_device, mesh=mesh, in_specs=placed, out_specs=P("layer", "row", "col"), check_vma=False
    )
```

```python
import jax
import jax.numpy as jnp
from jax import lax
from jax.experimental import pallas as pl
from jax.experimental.pallas import tpu as pltpu
from jax.sharding import PartitionSpec as P


BLOCK = 128
SUB = 32
KNEE = 32.0
STEEP = 1024.0
F32 = jnp.float32
BF16 = jnp.bfloat16
VMEM = pl.BlockSpec(memory_space=pltpu.VMEM)
SMEM = pl.BlockSpec(memory_space=pltpu.SMEM)
ANY = pl.BlockSpec(memory_space=pl.ANY)


def split(x):
    high = x.astype(BF16)
    return high, (x - high.astype(F32)).astype(BF16)


def dot(a, b):
    return jnp.dot(a, b, preferred_element_type=F32)


def dot3(a, b):
    return dot(a[0], b[0]) + (dot(a[0], b[1]) + dot(a[1], b[0]))


def code(v):
    return (v * jnp.clip(jnp.abs(v) * (1.0 / KNEE), 1.0 / STEEP, 1.0)).astype(BF16)


def decode(y):
    y = y.astype(F32)
    return y * jnp.clip(lax.rsqrt(jnp.abs(y) * (1.0 / KNEE)), 1.0, STEEP)


def here():
    layer = lax.axis_index("layer")
    return layer & 1, lax.axis_index("col"), lax.axis_index("row"), layer >> 1 & 3


def masked(tile, mask):
    return (tile.reshape(-1, *mask.shape) * mask[None]).reshape(tile.shape)


def grant(mebibytes):
    return pltpu.CompilerParams(vmem_limit_bytes=mebibytes * 1024 * 1024)


def cost(flops, moved):
    return pl.CostEstimate(flops=flops, bytes_accessed=moved, transcendentals=0)


def square_masks(order, width):
    rows = lax.broadcasted_iota(jnp.int32, (order, order), 0)
    cols = lax.broadcasted_iota(jnp.int32, (order, order), 1)
    return rows == cols, (rows < width) & (cols < width)


def place_kernel(in_ref, out_ref):
    for k in range(in_ref.shape[0]):
        out_ref[k] = in_ref[k]


def place_call(pos):
    return pl.pallas_call(
        place_kernel,
        in_specs=[SMEM],
        out_specs=SMEM,
        out_shape=jax.ShapeDtypeStruct(pos.shape, pos.dtype),
        cost_estimate=cost(10**10, 10**7),
        name="place",
        compiler_params=grant(1),
    )(pos)


def inverse_kernel(width_ref, pos_ref, system_ref, upper_ref, xh_ref, xl_ref, part_ref):
    members, order, _ = system_ref.shape
    half = upper_ref.shape[1]
    swap = pos_ref[2] == 1
    for s in range(members):
        on_diag, inside = square_masks(order, width_ref[s])
        identity = jnp.where(on_diag, 1.0, 0.0)
        system = jnp.where(inside, system_ref[s], identity)
        picked = jnp.where(on_diag, system, 0.0)
        down = 1.0 / jnp.sum(picked, axis=1, keepdims=True)
        across = 1.0 / jnp.sum(picked, axis=0, keepdims=True)
        start = jnp.where(on_diag, down, 0.0)
        inverse = (2.0 * start - down * (system * across)).astype(BF16)
        high, low = split(system)
        residual = identity - (dot(high, inverse) + dot(low, inverse))
        inverse = inverse.astype(F32) + dot(inverse, residual.astype(BF16))
        both = split(inverse)
        residual = identity - dot3((high, low), both)
        inverse = inverse + dot3(both, split(residual))
        inverse = jnp.where(inside, inverse, 0.0)
        mine = jnp.where(swap, inverse[:, half:], inverse[:, :half])
        other = jnp.where(swap, inverse[:, :half], inverse[:, half:])
        high, low = split(mine)
        upper = upper_ref[s]
        part_ref[s] = dot(high, upper) + dot(low, upper)
        high, low = split(other)
        xh_ref[s] = high
        xl_ref[s] = low


def inverse_call(widths, pos, systems, upper):
    members, order, _ = systems.shape
    half, cols = upper.shape[1:]
    return pl.pallas_call(
        inverse_kernel,
        in_specs=[SMEM, SMEM, VMEM, VMEM],
        out_specs=[VMEM] * 3,
        out_shape=[
            jax.ShapeDtypeStruct((members, order, half), BF16),
            jax.ShapeDtypeStruct((members, order, half), BF16),
            jax.ShapeDtypeStruct((members, order, cols), F32),
        ],
        cost_estimate=cost(14 * members * order**3, 8000000),
        name="inverse",
        compiler_params=grant(20),
    )(widths, pos, systems, upper)


def scale_kernel(mask_ref, xh_ref, xl_ref, part_ref, upper_ref, out_ref):
    members, order, cols = part_ref.shape
    pieces = order // BLOCK
    blocks = cols // BLOCK
    _, col, _, _ = here()
    for s in range(members):
        upper = upper_ref[s]
        scaled = part_ref[s] + (dot(xh_ref[s], upper) + dot(xl_ref[s], upper))
        for j in range(blocks):
            lanes = slice(j * BLOCK, (j + 1) * BLOCK)
            tile = masked(scaled[:, lanes].astype(BF16), mask_ref[s, col * blocks + j])
            for k in range(pieces):
                spot = lax.rem(k - col + pieces, pieces)
                out_ref[s, spot, :, lanes] = tile[k * BLOCK : (k + 1) * BLOCK]


def scale_call(masks, xh, xl, part, upper):
    members, order, half = xh.shape
    cols = upper.shape[2]
    return pl.pallas_call(
        scale_kernel,
        in_specs=[VMEM] * 5,
        out_specs=VMEM,
        out_shape=jax.ShapeDtypeStruct((members, order // BLOCK, BLOCK, cols), BF16),
        cost_estimate=cost(4 * members * order * half * cols, 8 * members * order * cols),
        name="scale_upper",
        compiler_params=grant(16),
    )(masks, xh, xl, part, upper)


def update_call(flip, chunk, masks, front, lowers, scaled, after):
    spots, _, _, rows, cols = front.shape
    members = scaled.shape[0]
    order = scaled.shape[1] * scaled.shape[2]

    def update_kernel(mask_ref, front_ref, *refs):
        own_ref, next_ref, last_ref, *far_refs, scaled_ref, _, out_ref, wide = refs
        core, _, row, _ = here()
        side = 1 - core if flip else core
        strip = 2 * rows
        base = row * (spots * 2 * strip) + side * strip + chunk * rows
        for s in range(members):
            for d in range(spots):
                for j in range(rows // SUB):
                    spot = lax.div(base + d * 2 * strip + j * SUB, BLOCK)
                    mask = mask_ref[s, spot]
                    spans = (d, side, slice(j * SUB, (j + 1) * SUB))
                    tiles = (own_ref[s, *spans], next_ref[s, *spans], far_refs[s][*spans], last_ref[s, *spans])
                    for k, tile in enumerate(tiles):
                        begin = s * order + k * BLOCK
                        top = d * rows + j * SUB
                        wide[top : top + SUB, begin : begin + BLOCK] = masked(tile, mask)
        flat = scaled_ref[...].reshape(members * order, cols)
        update = dot(wide[...], flat).reshape(spots, rows, cols)
        for d in range(spots):
            copy = front_ref[d, side, chunk].astype(F32) - update[d]
            out_ref[d] = code(copy) if flip else copy

    return pl.pallas_call(
        update_kernel,
        in_specs=[VMEM] * (len(lowers) + 3) + [ANY],
        out_specs=VMEM,
        scratch_shapes=[pltpu.VMEM((spots * rows, members * order), BF16)],
        out_shape=jax.ShapeDtypeStruct((spots, rows, cols), BF16 if flip else F32),
        cost_estimate=cost(2 * spots * rows * members * order * cols, 4000000),
        compiler_params=grant(12),
    )(masks, front, *lowers, scaled, after)


def fill_wide(wide, mask_ref, base, strip, tiles_of, spots, rows, members):
    for s in range(members):
        for d in range(spots):
            for j in range(rows // SUB):
                spot = lax.div(base + d * 2 * strip + j * SUB, BLOCK)
                mask = mask_ref[s, spot]
                top = d * rows + j * SUB
                for begin, tile in tiles_of(s, d, slice(j * SUB, (j + 1) * SUB)):
                    wide[top : top + SUB, begin : begin + BLOCK] = masked(tile, mask)


def joined(scaled_ref, piece):
    members = scaled_ref.shape[0]
    return jnp.concatenate([scaled_ref[s, piece] for s in range(members)], axis=0)


def near_call(chunk, masks, front, own, following, last, scaled, after):
    spots, sides, _, rows, cols = front.shape
    members, pieces = scaled.shape[:2]
    double = 2 * BLOCK

    def near_kernel(mask_ref, front_ref, own_ref, next_ref, last_ref, scaled_ref, _, out_ref, wide):
        strip = 2 * rows
        ends = joined(scaled_ref, pieces - 1)
        row = here()[2]
        for side in range(sides):
            base = row * (spots * 2 * strip) + side * strip + chunk * rows

            def tiles_of(s, d, span):
                where = (s, d, side, span)
                return (
                    (s * double, own_ref[where]),
                    (s * double + BLOCK, next_ref[where]),
                    (members * double + s * BLOCK, last_ref[where]),
                )

            fill_wide(wide, mask_ref, base, strip, tiles_of, spots, rows, members)
            total = dot(wide[:, members * double :], ends)
            for s in range(members):
                pair = scaled_ref[s, :2].reshape(double, cols)
                total = total + dot(wide[:, s * double : (s + 1) * double], pair)
            total = total.reshape(spots, rows, cols)
            for d in range(spots):
                out_ref[side, d] = front_ref[d, side, chunk].astype(F32) - total[d]

    return pl.pallas_call(
        near_kernel,
        in_specs=[VMEM] * 6 + [ANY],
        out_specs=VMEM,
        scratch_shapes=[pltpu.VMEM((spots * rows, members * 3 * BLOCK), BF16)],
        out_shape=jax.ShapeDtypeStruct((sides, spots, rows, cols), F32),
        cost_estimate=cost(4 * spots * rows * members * 3 * BLOCK * cols, 8000000),
        compiler_params=grant(14),
    )(masks, front, own, following, last, scaled, after)


def far_call(flip, chunk, masks, near, right, left, scaled):
    _, spots, rows, cols = near.shape
    members = scaled.shape[0]

    def far_kernel(mask_ref, near_ref, right_ref, left_ref, scaled_ref, out_ref, wide):
        core, _, row, _ = here()
        side = 1 - core if flip else core
        strip = 2 * rows
        base = row * (spots * 2 * strip) + side * strip + chunk * rows
        far_refs = (right_ref, left_ref)

        def tiles_of(s, d, span):
            return ((s * BLOCK, far_refs[s][d, side, span]),)

        fill_wide(wide, mask_ref, base, strip, tiles_of, spots, rows, members)
        total = dot(wide[...], joined(scaled_ref, 2)).reshape(spots, rows, cols)
        for d in range(spots):
            copy = near_ref[side, d] - total[d]
            out_ref[d] = code(copy) if flip else copy

    return pl.pallas_call(
        far_kernel,
        in_specs=[VMEM] * 5,
        out_specs=VMEM,
        scratch_shapes=[pltpu.VMEM((spots * rows, members * BLOCK), BF16)],
        out_shape=jax.ShapeDtypeStruct((spots, rows, cols), BF16 if flip else F32),
        cost_estimate=cost(2 * spots * rows * members * BLOCK * cols, 4000000),
        compiler_params=grant(12),
    )(masks, near, right, left, scaled)


def round_kernel(kept_ref, got_ref, *out_refs):
    place = here()[3]
    for k, out_ref in enumerate(out_refs):
        spot = lax.bitwise_xor(place, k + 1)
        out_ref[...] = code(kept_ref[spot] + decode(got_ref[spot]))


def round_call(kept, got):
    spots, rows, cols = kept.shape
    return pl.pallas_call(
        round_kernel,
        in_specs=[VMEM, VMEM],
        out_specs=[VMEM] * (spots - 1),
        out_shape=[jax.ShapeDtypeStruct((rows, cols), BF16)] * (spots - 1),
        cost_estimate=cost(spots * rows * cols, 10 * spots * rows * cols),
        compiler_params=grant(8),
    )(kept, got)


def chunk_kernel(kept_ref, core_ref, *refs):
    *got_refs, out_ref = refs
    place = here()[3]
    total = kept_ref[place] + decode(core_ref[place])
    for ref in got_refs:
        total = total + decode(ref[...])
    out_ref[...] = total


def chunk_call(kept, core, parts):
    _, rows, cols = kept.shape
    return pl.pallas_call(
        chunk_kernel,
        in_specs=[VMEM] * (len(parts) + 2),
        out_specs=VMEM,
        out_shape=jax.ShapeDtypeStruct((rows, cols), F32),
        cost_estimate=cost(len(parts) * rows * cols, 3 * len(parts) * rows * cols),
        compiler_params=grant(8),
    )(kept, core, *parts)


def final_kernel(early_ref, own_ref, *refs):
    *got_refs, out_ref = refs
    rows = own_ref.shape[0]
    out_ref[0, :rows] = early_ref[...]
    total = own_ref[...]
    for ref in got_refs:
        total = total + decode(ref[...])
    out_ref[0, rows:] = total


def final_call(early, parts):
    rows, cols = parts[0].shape
    return pl.pallas_call(
        final_kernel,
        in_specs=[VMEM] * (len(parts) + 1),
        out_specs=VMEM,
        out_shape=jax.ShapeDtypeStruct((1, 2 * rows, cols), F32),
        cost_estimate=cost(len(parts) * rows * cols, 3 * len(parts) * rows * cols),
        name="final_sums",
        compiler_params=grant(8),
    )(early, *parts)


def on_device(front_copies, lower_panels, upper_panels, diag_blocks, block_fill, widths):
    layers, col_devices = lax.axis_size("layer"), lax.axis_size("col")
    layer = lax.axis_index("layer")
    row_index, col_index = lax.axis_index("row"), lax.axis_index("col")
    which = jnp.arange(4, dtype=jnp.int32)
    pos = jnp.where(
        which == 0,
        layer & 1,
        jnp.where(which == 1, col_index, jnp.where(which == 2, row_index, layer >> 1 & 3)),
    ).astype(jnp.int32)
    pos = place_call(pos)
    upper, fill, width_vec = upper_panels[0], block_fill[0], widths[0]
    masks = jnp.broadcast_to(fill.astype(BF16)[:, :, None, None], (*fill.shape, 16, BLOCK))
    row_count, cols = front_copies.shape[1:]
    members = upper.shape[0]
    spots = 4
    rows = row_count // (spots * 4)
    front = front_copies.reshape(spots, 2, 2, rows, cols)
    lower = lower_panels.reshape(members, spots, 2, 2, rows, BLOCK)

    def shift(block, step):
        return lax.ppermute(block, "col", [(i, (i + step) % col_devices) for i in range(col_devices)])

    def across(block, flip):
        return lax.ppermute(block, "layer", [(i, i ^ flip) for i in range(layers)])

    other_upper = lax.ppermute(upper, "row", [(0, 1), (1, 0)])
    lowers = []
    for chunk in range(2):
        own = lower[:, :, :, chunk]
        following, last = shift(own, -1), shift(own, 1)
        right, left = shift(last[0], 1), shift(following[1], -1)
        lowers.append((own, following, last, right, left))
    xh, xl, part = inverse_call(width_vec, pos, diag_blocks[0], upper)
    scaled = scale_call(masks, xh, xl, part, other_upper)
    sums = []
    after = scaled
    for chunk in range(2):
        if chunk == 0:
            sent = update_call(True, chunk, masks, front, lowers[chunk], scaled, after)
        else:
            *near, right, left = lowers[chunk]
            near = near_call(chunk, masks, front, *near, scaled, after)
            sent = far_call(True, chunk, masks, near, right, left, scaled)
        core = across(sent, 1)
        if chunk == 0:
            kept = update_call(False, chunk, masks, front, lowers[chunk], scaled, after)
        else:
            kept = far_call(False, chunk, masks, near, right, left, scaled)
        one, two, three = round_call(kept, core)
        after = one
        parts = [across(two, 4), across(three, 6), across(one, 2)]
        if chunk == 0:
            sums.append(chunk_call(kept, core, parts))
        else:
            sums += [chunk_call(kept, core, []), *parts]
    return final_call(sums[0], sums[1:])


def solution(mesh):
    placed = (
        P("layer", "row", "col"),
        P("layer", None, "row", "col"),
        P("layer", None, "row", "col"),
        P("layer", None, None, None),
        P("layer", None, None),
        P("layer", None),
    )

    return jax.shard_map(
        on_device, mesh=mesh, in_specs=placed, out_specs=P("layer", "row", "col"), check_vma=False
    )
```

```python
import jax
import jax.numpy as jnp
from jax import lax
from jax.experimental import pallas as pl
from jax.experimental.pallas import tpu as pltpu
from jax.sharding import PartitionSpec as P


BLOCK = 128
SUB = 32
KNEE = 32.0
STEEP = 1024.0
F32 = jnp.float32
BF16 = jnp.bfloat16
VMEM = pl.BlockSpec(memory_space=pltpu.VMEM)
SMEM = pl.BlockSpec(memory_space=pltpu.SMEM)
ANY = pl.BlockSpec(memory_space=pl.ANY)


def split(x):
    high = x.astype(BF16)
    return high, (x - high.astype(F32)).astype(BF16)


def dot(a, b):
    return jnp.dot(a, b, preferred_element_type=F32)


def dot3(a, b):
    return dot(a[0], b[0]) + (dot(a[0], b[1]) + dot(a[1], b[0]))


def code(v):
    return (v * jnp.clip(jnp.abs(v) * (1.0 / KNEE), 1.0 / STEEP, 1.0)).astype(BF16)


def decode(y):
    y = y.astype(F32)
    return y * jnp.clip(lax.rsqrt(jnp.abs(y) * (1.0 / KNEE)), 1.0, STEEP)


def here():
    layer = lax.axis_index("layer")
    return layer & 1, lax.axis_index("col"), lax.axis_index("row"), layer >> 1 & 3


def masked(tile, mask):
    return (tile.reshape(-1, *mask.shape) * mask[None]).reshape(tile.shape)


def grant(mebibytes):
    return pltpu.CompilerParams(vmem_limit_bytes=mebibytes * 1024 * 1024)


def cost(flops, moved):
    return pl.CostEstimate(flops=flops, bytes_accessed=moved, transcendentals=0)


def square_masks(order, width):
    rows = lax.broadcasted_iota(jnp.int32, (order, order), 0)
    cols = lax.broadcasted_iota(jnp.int32, (order, order), 1)
    return rows == cols, (rows < width) & (cols < width)


def place_kernel(out_ref):
    out_ref[...] = jnp.zeros_like(out_ref)


def place_call():
    return pl.pallas_call(
        place_kernel,
        in_specs=[],
        out_specs=VMEM,
        out_shape=jax.ShapeDtypeStruct((8, BLOCK), F32),
        cost_estimate=cost(10**10, 10**7),
        name="place",
        compiler_params=grant(1),
    )()


def inverse_kernel(width_ref, system_ref, upper_ref, _, xh_ref, xl_ref, part_ref):
    members, order, _ = system_ref.shape
    half = upper_ref.shape[1]
    swap = lax.axis_index("row") == 1
    for s in range(members):
        on_diag, inside = square_masks(order, width_ref[s])
        identity = jnp.where(on_diag, 1.0, 0.0)
        system = jnp.where(inside, system_ref[s], identity)
        picked = jnp.where(on_diag, system, 0.0)
        down = 1.0 / jnp.sum(picked, axis=1, keepdims=True)
        across = 1.0 / jnp.sum(picked, axis=0, keepdims=True)
        start = jnp.where(on_diag, down, 0.0)
        inverse = (2.0 * start - down * (system * across)).astype(BF16)
        high, low = split(system)
        residual = identity - (dot(high, inverse) + dot(low, inverse))
        inverse = inverse.astype(F32) + dot(inverse, residual.astype(BF16))
        both = split(inverse)
        residual = identity - dot3((high, low), both)
        inverse = inverse + dot3(both, split(residual))
        inverse = jnp.where(inside, inverse, 0.0)
        mine = jnp.where(swap, inverse[:, half:], inverse[:, :half])
        other = jnp.where(swap, inverse[:, :half], inverse[:, half:])
        high, low = split(mine)
        upper = upper_ref[s]
        part_ref[s] = dot(high, upper) + dot(low, upper)
        high, low = split(other)
        xh_ref[s] = high
        xl_ref[s] = low


def inverse_call(widths, systems, upper, mark):
    members, order, _ = systems.shape
    half, cols = upper.shape[1:]
    return pl.pallas_call(
        inverse_kernel,
        in_specs=[SMEM, VMEM, VMEM, ANY],
        out_specs=[VMEM] * 3,
        out_shape=[
            jax.ShapeDtypeStruct((members, order, half), BF16),
            jax.ShapeDtypeStruct((members, order, half), BF16),
            jax.ShapeDtypeStruct((members, order, cols), F32),
        ],
        cost_estimate=cost(14 * members * order**3, 8000000),
        name="inverse",
        compiler_params=grant(20),
    )(widths, systems, upper, mark)


def scale_kernel(mask_ref, xh_ref, xl_ref, part_ref, upper_ref, out_ref):
    members, order, cols = part_ref.shape
    pieces = order // BLOCK
    blocks = cols // BLOCK
    _, col, _, _ = here()
    for s in range(members):
        upper = upper_ref[s]
        scaled = part_ref[s] + (dot(xh_ref[s], upper) + dot(xl_ref[s], upper))
        for j in range(blocks):
            lanes = slice(j * BLOCK, (j + 1) * BLOCK)
            tile = masked(scaled[:, lanes].astype(BF16), mask_ref[s, col * blocks + j])
            for k in range(pieces):
                spot = lax.rem(k - col + pieces, pieces)
                out_ref[s, spot, :, lanes] = tile[k * BLOCK : (k + 1) * BLOCK]


def scale_call(masks, xh, xl, part, upper):
    members, order, half = xh.shape
    cols = upper.shape[2]
    return pl.pallas_call(
        scale_kernel,
        in_specs=[VMEM] * 5,
        out_specs=VMEM,
        out_shape=jax.ShapeDtypeStruct((members, order // BLOCK, BLOCK, cols), BF16),
        cost_estimate=cost(4 * members * order * half * cols, 8 * members * order * cols),
        name="scale_upper",
        compiler_params=grant(16),
    )(masks, xh, xl, part, upper)


def update_call(flip, chunk, masks, front, lowers, scaled, after):
    spots, _, _, rows, cols = front.shape
    members = scaled.shape[0]
    order = scaled.shape[1] * scaled.shape[2]

    def update_kernel(mask_ref, front_ref, *refs):
        own_ref, next_ref, last_ref, *far_refs, scaled_ref, _, out_ref, wide = refs
        core, _, row, _ = here()
        side = 1 - core if flip else core
        strip = 2 * rows
        base = row * (spots * 2 * strip) + side * strip + chunk * rows
        for s in range(members):
            for d in range(spots):
                for j in range(rows // SUB):
                    spot = lax.div(base + d * 2 * strip + j * SUB, BLOCK)
                    mask = mask_ref[s, spot]
                    spans = (d, side, slice(j * SUB, (j + 1) * SUB))
                    tiles = (own_ref[s, *spans], next_ref[s, *spans], far_refs[s][*spans], last_ref[s, *spans])
                    for k, tile in enumerate(tiles):
                        begin = s * order + k * BLOCK
                        top = d * rows + j * SUB
                        wide[top : top + SUB, begin : begin + BLOCK] = masked(tile, mask)
        flat = scaled_ref[...].reshape(members * order, cols)
        update = dot(wide[...], flat).reshape(spots, rows, cols)
        for d in range(spots):
            copy = front_ref[d, side, chunk].astype(F32) - update[d]
            out_ref[d] = code(copy) if flip else copy

    return pl.pallas_call(
        update_kernel,
        in_specs=[VMEM] * (len(lowers) + 3) + [ANY],
        out_specs=VMEM,
        scratch_shapes=[pltpu.VMEM((spots * rows, members * order), BF16)],
        out_shape=jax.ShapeDtypeStruct((spots, rows, cols), BF16 if flip else F32),
        cost_estimate=cost(2 * spots * rows * members * order * cols, 4000000),
        compiler_params=grant(12),
    )(masks, front, *lowers, scaled, after)


def fill_wide(wide, mask_ref, base, strip, tiles_of, spots, rows, members):
    for s in range(members):
        for d in range(spots):
            for j in range(rows // SUB):
                spot = lax.div(base + d * 2 * strip + j * SUB, BLOCK)
                mask = mask_ref[s, spot]
                top = d * rows + j * SUB
                for begin, tile in tiles_of(s, d, slice(j * SUB, (j + 1) * SUB)):
                    wide[top : top + SUB, begin : begin + BLOCK] = masked(tile, mask)


def joined(scaled_ref, piece):
    members = scaled_ref.shape[0]
    return jnp.concatenate([scaled_ref[s, piece] for s in range(members)], axis=0)


def near_call(chunk, masks, front, own, following, last, scaled, after):
    spots, sides, _, rows, cols = front.shape
    members, pieces = scaled.shape[:2]
    double = 2 * BLOCK

    def near_kernel(mask_ref, front_ref, own_ref, next_ref, last_ref, scaled_ref, _, out_ref, wide):
        strip = 2 * rows
        ends = joined(scaled_ref, pieces - 1)
        row = here()[2]
        for side in range(sides):
            base = row * (spots * 2 * strip) + side * strip + chunk * rows

            def tiles_of(s, d, span):
                where = (s, d, side, span)
                return (
                    (s * double, own_ref[where]),
                    (s * double + BLOCK, next_ref[where]),
                    (members * double + s * BLOCK, last_ref[where]),
                )

            fill_wide(wide, mask_ref, base, strip, tiles_of, spots, rows, members)
            total = dot(wide[:, members * double :], ends)
            for s in range(members):
                pair = scaled_ref[s, :2].reshape(double, cols)
                total = total + dot(wide[:, s * double : (s + 1) * double], pair)
            total = total.reshape(spots, rows, cols)
            for d in range(spots):
                out_ref[side, d] = front_ref[d, side, chunk].astype(F32) - total[d]

    return pl.pallas_call(
        near_kernel,
        in_specs=[VMEM] * 6 + [ANY],
        out_specs=VMEM,
        scratch_shapes=[pltpu.VMEM((spots * rows, members * 3 * BLOCK), BF16)],
        out_shape=jax.ShapeDtypeStruct((sides, spots, rows, cols), F32),
        cost_estimate=cost(4 * spots * rows * members * 3 * BLOCK * cols, 8000000),
        compiler_params=grant(14),
    )(masks, front, own, following, last, scaled, after)


def far_call(flip, chunk, masks, near, right, left, scaled):
    _, spots, rows, cols = near.shape
    members = scaled.shape[0]

    def far_kernel(mask_ref, near_ref, right_ref, left_ref, scaled_ref, out_ref, wide):
        core, _, row, _ = here()
        side = 1 - core if flip else core
        strip = 2 * rows
        base = row * (spots * 2 * strip) + side * strip + chunk * rows
        far_refs = (right_ref, left_ref)

        def tiles_of(s, d, span):
            return ((s * BLOCK, far_refs[s][d, side, span]),)

        fill_wide(wide, mask_ref, base, strip, tiles_of, spots, rows, members)
        total = dot(wide[...], joined(scaled_ref, 2)).reshape(spots, rows, cols)
        for d in range(spots):
            copy = near_ref[side, d] - total[d]
            out_ref[d] = code(copy) if flip else copy

    return pl.pallas_call(
        far_kernel,
        in_specs=[VMEM] * 5,
        out_specs=VMEM,
        scratch_shapes=[pltpu.VMEM((spots * rows, members * BLOCK), BF16)],
        out_shape=jax.ShapeDtypeStruct((spots, rows, cols), BF16 if flip else F32),
        cost_estimate=cost(2 * spots * rows * members * BLOCK * cols, 4000000),
        compiler_params=grant(12),
    )(masks, near, right, left, scaled)


def round_kernel(kept_ref, got_ref, *out_refs):
    place = here()[3]
    for k, out_ref in enumerate(out_refs):
        spot = lax.bitwise_xor(place, k + 1)
        out_ref[...] = code(kept_ref[spot] + decode(got_ref[spot]))


def round_call(kept, got):
    spots, rows, cols = kept.shape
    return pl.pallas_call(
        round_kernel,
        in_specs=[VMEM, VMEM],
        out_specs=[VMEM] * (spots - 1),
        out_shape=[jax.ShapeDtypeStruct((rows, cols), BF16)] * (spots - 1),
        cost_estimate=cost(spots * rows * cols, 10 * spots * rows * cols),
        compiler_params=grant(8),
    )(kept, got)


def chunk_kernel(kept_ref, core_ref, *refs):
    *got_refs, out_ref = refs
    place = here()[3]
    total = kept_ref[place] + decode(core_ref[place])
    for ref in got_refs:
        total = total + decode(ref[...])
    out_ref[...] = total


def chunk_call(kept, core, parts):
    _, rows, cols = kept.shape
    return pl.pallas_call(
        chunk_kernel,
        in_specs=[VMEM] * (len(parts) + 2),
        out_specs=VMEM,
        out_shape=jax.ShapeDtypeStruct((rows, cols), F32),
        cost_estimate=cost(len(parts) * rows * cols, 3 * len(parts) * rows * cols),
        compiler_params=grant(8),
    )(kept, core, *parts)


def final_kernel(early_ref, own_ref, *refs):
    *got_refs, out_ref = refs
    rows = own_ref.shape[0]
    out_ref[0, :rows] = early_ref[...]
    total = own_ref[...]
    for ref in got_refs:
        total = total + decode(ref[...])
    out_ref[0, rows:] = total


def final_call(early, parts):
    rows, cols = parts[0].shape
    return pl.pallas_call(
        final_kernel,
        in_specs=[VMEM] * (len(parts) + 1),
        out_specs=VMEM,
        out_shape=jax.ShapeDtypeStruct((1, 2 * rows, cols), F32),
        cost_estimate=cost(len(parts) * rows * cols, 3 * len(parts) * rows * cols),
        name="final_sums",
        compiler_params=grant(8),
    )(early, *parts)


def on_device(front_copies, lower_panels, upper_panels, diag_blocks, block_fill, widths):
    layers, col_devices = lax.axis_size("layer"), lax.axis_size("col")
    upper, fill, width_vec = upper_panels[0], block_fill[0], widths[0]
    masks = jnp.broadcast_to(fill.astype(BF16)[:, :, None, None], (*fill.shape, 16, BLOCK))
    row_count, cols = front_copies.shape[1:]
    members = upper.shape[0]
    spots = 4
    rows = row_count // (spots * 4)
    front = front_copies.reshape(spots, 2, 2, rows, cols)
    lower = lower_panels.reshape(members, spots, 2, 2, rows, BLOCK)

    def shift(block, step):
        return lax.ppermute(block, "col", [(i, (i + step) % col_devices) for i in range(col_devices)])

    def across(block, flip):
        return lax.ppermute(block, "layer", [(i, i ^ flip) for i in range(layers)])

    other_upper = lax.ppermute(upper, "row", [(0, 1), (1, 0)])
    lowers = []
    for chunk in range(2):
        own = lower[:, :, :, chunk]
        following, last = shift(own, -1), shift(own, 1)
        right, left = shift(last[0], 1), shift(following[1], -1)
        lowers.append((own, following, last, right, left))
    xh, xl, part = inverse_call(width_vec, diag_blocks[0], upper, place_call())
    scaled = scale_call(masks, xh, xl, part, other_upper)
    sums = []
    after = scaled
    for chunk in range(2):
        if chunk == 0:
            sent = update_call(True, chunk, masks, front, lowers[chunk], scaled, after)
        else:
            *near, right, left = lowers[chunk]
            near = near_call(chunk, masks, front, *near, scaled, after)
            sent = far_call(True, chunk, masks, near, right, left, scaled)
        core = across(sent, 1)
        if chunk == 0:
            kept = update_call(False, chunk, masks, front, lowers[chunk], scaled, after)
        else:
            kept = far_call(False, chunk, masks, near, right, left, scaled)
        one, two, three = round_call(kept, core)
        after = one
        parts = [across(two, 4), across(three, 6), across(one, 2)]
        if chunk == 0:
            sums.append(chunk_call(kept, core, parts))
        else:
            sums += [chunk_call(kept, core, []), *parts]
    return final_call(sums[0], sums[1:])


def solution(mesh):
    placed = (
        P("layer", "row", "col"),
        P("layer", None, "row", "col"),
        P("layer", None, "row", "col"),
        P("layer", None, None, None),
        P("layer", None, None),
        P("layer", None),
    )

    return jax.shard_map(
        on_device, mesh=mesh, in_specs=placed, out_specs=P("layer", "row", "col"), check_vma=False
    )
```

```python
import jax
import jax.numpy as jnp
from jax import lax
from jax.experimental import pallas as pl
from jax.experimental.pallas import tpu as pltpu
from jax.sharding import PartitionSpec as P


BLOCK = 128
SUB = 32
KNEE = 32.0
STEEP = 1024.0
F32 = jnp.float32
BF16 = jnp.bfloat16
VMEM = pl.BlockSpec(memory_space=pltpu.VMEM)
SMEM = pl.BlockSpec(memory_space=pltpu.SMEM)
ANY = pl.BlockSpec(memory_space=pl.ANY)


def split(x):
    high = x.astype(BF16)
    return high, (x - high.astype(F32)).astype(BF16)


def dot(a, b):
    return jnp.dot(a, b, preferred_element_type=F32)


def dot3(a, b):
    return dot(a[0], b[0]) + (dot(a[0], b[1]) + dot(a[1], b[0]))


def code(v):
    return (v * jnp.clip(jnp.abs(v) * (1.0 / KNEE), 1.0 / STEEP, 1.0)).astype(BF16)


def decode(y):
    y = y.astype(F32)
    return y * jnp.clip(lax.rsqrt(jnp.abs(y) * (1.0 / KNEE)), 1.0, STEEP)


def here():
    layer = lax.axis_index("layer")
    return layer & 1, lax.axis_index("col"), lax.axis_index("row"), layer >> 1 & 3


def masked(tile, mask):
    return (tile.reshape(-1, *mask.shape) * mask[None]).reshape(tile.shape)


def grant(mebibytes):
    return pltpu.CompilerParams(vmem_limit_bytes=mebibytes * 1024 * 1024)


def cost(flops, moved):
    return pl.CostEstimate(flops=flops, bytes_accessed=moved, transcendentals=0)


def square_masks(order, width):
    rows = lax.broadcasted_iota(jnp.int32, (order, order), 0)
    cols = lax.broadcasted_iota(jnp.int32, (order, order), 1)
    return rows == cols, (rows < width) & (cols < width)


def place_kernel(out_ref):
    out_ref[...] = jnp.zeros_like(out_ref)


def place_call():
    return pl.pallas_call(
        place_kernel,
        in_specs=[],
        out_specs=VMEM,
        out_shape=jax.ShapeDtypeStruct((8, BLOCK), F32),
        cost_estimate=cost(10**10, 10**7),
        name="place",
        compiler_params=grant(1),
    )()


def inverse_kernel(width_ref, system_ref, upper_ref, mark_ref, front_ref, xh_ref, xl_ref, part_ref):
    members, order, _ = system_ref.shape
    half = upper_ref.shape[1]
    swap = lax.axis_index("row") == 1
    for s in range(members):
        on_diag, inside = square_masks(order, width_ref[s])
        identity = jnp.where(on_diag, 1.0, 0.0)
        system = jnp.where(inside, system_ref[s], identity)
        picked = jnp.where(on_diag, system, 0.0)
        down = 1.0 / jnp.sum(picked, axis=1, keepdims=True)
        across = 1.0 / jnp.sum(picked, axis=0, keepdims=True)
        start = jnp.where(on_diag, down, 0.0)
        inverse = (2.0 * start - down * (system * across)).astype(BF16)
        high, low = split(system)
        residual = identity - (dot(high, inverse) + dot(low, inverse))
        inverse = inverse.astype(F32) + dot(inverse, residual.astype(BF16))
        both = split(inverse)
        residual = identity - dot3((high, low), both)
        inverse = inverse + dot3(both, split(residual))
        inverse = jnp.where(inside, inverse, 0.0)
        mine = jnp.where(swap, inverse[:, half:], inverse[:, :half])
        other = jnp.where(swap, inverse[:, :half], inverse[:, half:])
        high, low = split(mine)
        upper = upper_ref[s]
        part_ref[s] = dot(high, upper) + dot(low, upper)
        high, low = split(other)
        xh_ref[s] = high
        xl_ref[s] = low


def inverse_call(widths, systems, upper, mark, front):
    members, order, _ = systems.shape
    half, cols = upper.shape[1:]
    return pl.pallas_call(
        inverse_kernel,
        in_specs=[SMEM, VMEM, VMEM, ANY, VMEM],
        out_specs=[VMEM] * 3,
        out_shape=[
            jax.ShapeDtypeStruct((members, order, half), BF16),
            jax.ShapeDtypeStruct((members, order, half), BF16),
            jax.ShapeDtypeStruct((members, order, cols), F32),
        ],
        cost_estimate=cost(14 * members * order**3, 8000000),
        name="inverse",
        compiler_params=grant(20),
    )(widths, systems, upper, mark, front)


def scale_kernel(mask_ref, xh_ref, xl_ref, part_ref, upper_ref, out_ref):
    members, order, cols = part_ref.shape
    pieces = order // BLOCK
    blocks = cols // BLOCK
    _, col, _, _ = here()
    for s in range(members):
        upper = upper_ref[s]
        scaled = part_ref[s] + (dot(xh_ref[s], upper) + dot(xl_ref[s], upper))
        for j in range(blocks):
            lanes = slice(j * BLOCK, (j + 1) * BLOCK)
            tile = masked(scaled[:, lanes].astype(BF16), mask_ref[s, col * blocks + j])
            for k in range(pieces):
                spot = lax.rem(k - col + pieces, pieces)
                out_ref[s, spot, :, lanes] = tile[k * BLOCK : (k + 1) * BLOCK]


def scale_call(masks, xh, xl, part, upper):
    members, order, half = xh.shape
    cols = upper.shape[2]
    return pl.pallas_call(
        scale_kernel,
        in_specs=[VMEM] * 5,
        out_specs=VMEM,
        out_shape=jax.ShapeDtypeStruct((members, order // BLOCK, BLOCK, cols), BF16),
        cost_estimate=cost(4 * members * order * half * cols, 8 * members * order * cols),
        name="scale_upper",
        compiler_params=grant(16),
    )(masks, xh, xl, part, upper)


def update_call(flip, chunk, masks, front, lowers, scaled, after):
    spots, _, _, rows, cols = front.shape
    members = scaled.shape[0]
    order = scaled.shape[1] * scaled.shape[2]

    def update_kernel(mask_ref, front_ref, *refs):
        own_ref, next_ref, last_ref, *far_refs, scaled_ref, _, out_ref, wide = refs
        core, _, row, _ = here()
        side = 1 - core if flip else core
        strip = 2 * rows
        base = row * (spots * 2 * strip) + side * strip + chunk * rows
        for s in range(members):
            for d in range(spots):
                for j in range(rows // SUB):
                    spot = lax.div(base + d * 2 * strip + j * SUB, BLOCK)
                    mask = mask_ref[s, spot]
                    spans = (d, side, slice(j * SUB, (j + 1) * SUB))
                    tiles = (own_ref[s, *spans], next_ref[s, *spans], far_refs[s][*spans], last_ref[s, *spans])
                    for k, tile in enumerate(tiles):
                        begin = s * order + k * BLOCK
                        top = d * rows + j * SUB
                        wide[top : top + SUB, begin : begin + BLOCK] = masked(tile, mask)
        flat = scaled_ref[...].reshape(members * order, cols)
        update = dot(wide[...], flat).reshape(spots, rows, cols)
        for d in range(spots):
            copy = front_ref[d, side, chunk].astype(F32) - update[d]
            out_ref[d] = code(copy) if flip else copy

    return pl.pallas_call(
        update_kernel,
        in_specs=[VMEM] * (len(lowers) + 3) + [ANY],
        out_specs=VMEM,
        scratch_shapes=[pltpu.VMEM((spots * rows, members * order), BF16)],
        out_shape=jax.ShapeDtypeStruct((spots, rows, cols), BF16 if flip else F32),
        cost_estimate=cost(2 * spots * rows * members * order * cols, 4000000),
        compiler_params=grant(12),
    )(masks, front, *lowers, scaled, after)


def fill_wide(wide, mask_ref, base, strip, tiles_of, spots, rows, members):
    for s in range(members):
        for d in range(spots):
            for j in range(rows // SUB):
                spot = lax.div(base + d * 2 * strip + j * SUB, BLOCK)
                mask = mask_ref[s, spot]
                top = d * rows + j * SUB
                for begin, tile in tiles_of(s, d, slice(j * SUB, (j + 1) * SUB)):
                    wide[top : top + SUB, begin : begin + BLOCK] = masked(tile, mask)


def joined(scaled_ref, piece):
    members = scaled_ref.shape[0]
    return jnp.concatenate([scaled_ref[s, piece] for s in range(members)], axis=0)


def near_call(chunk, masks, front, own, following, last, scaled, after):
    spots, sides, _, rows, cols = front.shape
    members, pieces = scaled.shape[:2]
    double = 2 * BLOCK

    def near_kernel(mask_ref, front_ref, own_ref, next_ref, last_ref, scaled_ref, _, out_ref, wide):
        strip = 2 * rows
        ends = joined(scaled_ref, pieces - 1)
        row = here()[2]
        for side in range(sides):
            base = row * (spots * 2 * strip) + side * strip + chunk * rows

            def tiles_of(s, d, span):
                where = (s, d, side, span)
                return (
                    (s * double, own_ref[where]),
                    (s * double + BLOCK, next_ref[where]),
                    (members * double + s * BLOCK, last_ref[where]),
                )

            fill_wide(wide, mask_ref, base, strip, tiles_of, spots, rows, members)
            total = dot(wide[:, members * double :], ends)
            for s in range(members):
                pair = scaled_ref[s, :2].reshape(double, cols)
                total = total + dot(wide[:, s * double : (s + 1) * double], pair)
            total = total.reshape(spots, rows, cols)
            for d in range(spots):
                out_ref[side, d] = front_ref[d, side, chunk].astype(F32) - total[d]

    return pl.pallas_call(
        near_kernel,
        in_specs=[VMEM] * 6 + [ANY],
        out_specs=VMEM,
        scratch_shapes=[pltpu.VMEM((spots * rows, members * 3 * BLOCK), BF16)],
        out_shape=jax.ShapeDtypeStruct((sides, spots, rows, cols), F32),
        cost_estimate=cost(4 * spots * rows * members * 3 * BLOCK * cols, 8000000),
        compiler_params=grant(14),
    )(masks, front, own, following, last, scaled, after)


def far_call(flip, chunk, masks, near, right, left, scaled):
    _, spots, rows, cols = near.shape
    members = scaled.shape[0]

    def far_kernel(mask_ref, near_ref, right_ref, left_ref, scaled_ref, out_ref, wide):
        core, _, row, _ = here()
        side = 1 - core if flip else core
        strip = 2 * rows
        base = row * (spots * 2 * strip) + side * strip + chunk * rows
        far_refs = (right_ref, left_ref)

        def tiles_of(s, d, span):
            return ((s * BLOCK, far_refs[s][d, side, span]),)

        fill_wide(wide, mask_ref, base, strip, tiles_of, spots, rows, members)
        total = dot(wide[...], joined(scaled_ref, 2)).reshape(spots, rows, cols)
        for d in range(spots):
            copy = near_ref[side, d] - total[d]
            out_ref[d] = code(copy) if flip else copy

    return pl.pallas_call(
        far_kernel,
        in_specs=[VMEM] * 5,
        out_specs=VMEM,
        scratch_shapes=[pltpu.VMEM((spots * rows, members * BLOCK), BF16)],
        out_shape=jax.ShapeDtypeStruct((spots, rows, cols), BF16 if flip else F32),
        cost_estimate=cost(2 * spots * rows * members * BLOCK * cols, 4000000),
        compiler_params=grant(12),
    )(masks, near, right, left, scaled)


def round_kernel(kept_ref, got_ref, *out_refs):
    place = here()[3]
    for k, out_ref in enumerate(out_refs):
        spot = lax.bitwise_xor(place, k + 1)
        out_ref[...] = code(kept_ref[spot] + decode(got_ref[spot]))


def round_call(kept, got):
    spots, rows, cols = kept.shape
    return pl.pallas_call(
        round_kernel,
        in_specs=[VMEM, VMEM],
        out_specs=[VMEM] * (spots - 1),
        out_shape=[jax.ShapeDtypeStruct((rows, cols), BF16)] * (spots - 1),
        cost_estimate=cost(spots * rows * cols, 10 * spots * rows * cols),
        compiler_params=grant(8),
    )(kept, got)


def chunk_kernel(kept_ref, core_ref, *refs):
    *got_refs, out_ref = refs
    place = here()[3]
    total = kept_ref[place] + decode(core_ref[place])
    for ref in got_refs:
        total = total + decode(ref[...])
    out_ref[...] = total


def chunk_call(kept, core, parts):
    _, rows, cols = kept.shape
    return pl.pallas_call(
        chunk_kernel,
        in_specs=[VMEM] * (len(parts) + 2),
        out_specs=VMEM,
        out_shape=jax.ShapeDtypeStruct((rows, cols), F32),
        cost_estimate=cost(len(parts) * rows * cols, 3 * len(parts) * rows * cols),
        compiler_params=grant(8),
    )(kept, core, *parts)


def final_kernel(early_ref, own_ref, *refs):
    *got_refs, out_ref = refs
    rows = own_ref.shape[0]
    out_ref[0, :rows] = early_ref[...]
    total = own_ref[...]
    for ref in got_refs:
        total = total + decode(ref[...])
    out_ref[0, rows:] = total


def final_call(early, parts):
    rows, cols = parts[0].shape
    return pl.pallas_call(
        final_kernel,
        in_specs=[VMEM] * (len(parts) + 1),
        out_specs=VMEM,
        out_shape=jax.ShapeDtypeStruct((1, 2 * rows, cols), F32),
        cost_estimate=cost(len(parts) * rows * cols, 3 * len(parts) * rows * cols),
        name="final_sums",
        compiler_params=grant(8),
    )(early, *parts)


def on_device(front_copies, lower_panels, upper_panels, diag_blocks, block_fill, widths):
    layers, col_devices = lax.axis_size("layer"), lax.axis_size("col")
    upper, fill, width_vec = upper_panels[0], block_fill[0], widths[0]
    masks = jnp.broadcast_to(fill.astype(BF16)[:, :, None, None], (*fill.shape, 16, BLOCK))
    row_count, cols = front_copies.shape[1:]
    members = upper.shape[0]
    spots = 4
    rows = row_count // (spots * 4)
    front = front_copies.reshape(spots, 2, 2, rows, cols)
    lower = lower_panels.reshape(members, spots, 2, 2, rows, BLOCK)

    def shift(block, step):
        return lax.ppermute(block, "col", [(i, (i + step) % col_devices) for i in range(col_devices)])

    def across(block, flip):
        return lax.ppermute(block, "layer", [(i, i ^ flip) for i in range(layers)])

    other_upper = lax.ppermute(upper, "row", [(0, 1), (1, 0)])
    lowers = []
    for chunk in range(2):
        own = lower[:, :, :, chunk]
        following, last = shift(own, -1), shift(own, 1)
        right, left = shift(last[0], 1), shift(following[1], -1)
        lowers.append((own, following, last, right, left))
    xh, xl, part = inverse_call(width_vec, diag_blocks[0], upper, place_call(), front)
    scaled = scale_call(masks, xh, xl, part, other_upper)
    sums = []
    after = scaled
    for chunk in range(2):
        if chunk == 0:
            sent = update_call(True, chunk, masks, front, lowers[chunk], scaled, after)
        else:
            *near, right, left = lowers[chunk]
            near = near_call(chunk, masks, front, *near, scaled, after)
            sent = far_call(True, chunk, masks, near, right, left, scaled)
        core = across(sent, 1)
        if chunk == 0:
            kept = update_call(False, chunk, masks, front, lowers[chunk], scaled, after)
        else:
            kept = far_call(False, chunk, masks, near, right, left, scaled)
        one, two, three = round_call(kept, core)
        after = one
        parts = [across(two, 4), across(three, 6), across(one, 2)]
        if chunk == 0:
            sums.append(chunk_call(kept, core, parts))
        else:
            sums += [chunk_call(kept, core, []), *parts]
    return final_call(sums[0], sums[1:])


def solution(mesh):
    placed = (
        P("layer", "row", "col"),
        P("layer", None, "row", "col"),
        P("layer", None, "row", "col"),
        P("layer", None, None, None),
        P("layer", None, None),
        P("layer", None),
    )

    return jax.shard_map(
        on_device, mesh=mesh, in_specs=placed, out_specs=P("layer", "row", "col"), check_vma=False
    )
```
